256 devices in a mesh: ctx: 32 (over y, x, core), head: 8 (over z).
Axes of the slice: x: 4, y: 4, z: 8, core: 2. Of those that a mesh axis runs over, the one named last changes fastest.
Arguments:
- query_rows: bfloat16 [32768, 4096], P('ctx', 'head'), may hold values from -6 to 6
- key_rows: bfloat16 [32768, 4096], P('ctx', 'head'), may hold values from -6 to 6
- value_rows: bfloat16 [32768, 4096], P('ctx', 'head'), may hold values from -6 to 6
- frequencies: bfloat16 [32, 128, 128], P('head'), may hold values from -4.1875 to 4.1875
- norm_gain: bfloat16 [4096], P('head'), may hold values from 0.25 to 1.75
- out_weight: bfloat16 [4096, 4096], P(None, 'head'), may hold values from -0.09375 to 0.09375
Outputs:
- projected: bfloat16 [32768, 4096], P('ctx', 'head')
The draws below stay inside these ranges and needn't reach their ends.
All inputs are finite; a program needn't handle non-finite values.
Results may differ from the reference program's by a relative error of at most 0.009.
Values may be sent and summed in bfloat16 or wider, within the bound.
A program may use at most 128 MiB of HBM per device.

```python
import math
import jax
import jax.numpy as jnp
from jax import lax

D = 4096
HEADS = 32
HDIM = 128
NFREQ = 128
FEATS = 256
BLOCK = 512
SEQ_LEN = 32768


def block_scale(key, shape, cuts, least, top_value):
    gain = 1.0
    for dim, parts in cuts:
        steps = jax.random.uniform(jax.random.fold_in(jax.random.fold_in(key, 6), dim), (parts,), jnp.float32, least / len(cuts), top_value / len(cuts))
        gain = gain * jnp.repeat(jnp.exp(steps), shape[dim] // parts).reshape((-1,) + (1,) * (len(shape) - 1 - dim))
    return gain


def normal_values(key, shape, deviation, most, cuts=(), dtype=jnp.bfloat16):
    level = block_scale(key, shape, cuts, -0.22, 0.18) if cuts else 1.0
    result = jax.random.normal(key, shape, jnp.float32) * deviation * level
    return jnp.minimum(jnp.maximum(result, -most), most).astype(dtype)


def setup_inputs(seed: int = 0) -> dict:
    key_list = jax.random.split(jax.random.key(seed), 7)
    query_rows = normal_values(key_list[0], (SEQ_LEN, HEADS * HDIM), 1.0, 6.0, ((0, 32), (1, 8)))
    key_rows = normal_values(key_list[1], (SEQ_LEN, HEADS * HDIM), 1.0, 6.0, ((0, 32), (1, 8)))
    value_rows = normal_values(key_list[2], (SEQ_LEN, HEADS * HDIM), 1.0, 6.0, ((0, 32), (1, 8)))
    frequencies = normal_values(key_list[3], (HEADS, HDIM, NFREQ), 0.7, 4.1875, ((0, 8),))
    norm_gain = jnp.clip(1.0 + 0.15 * jax.random.normal(key_list[4], (HEADS * HDIM,), jnp.float32), 0.25, 1.75).astype(jnp.bfloat16)
    out_weight = normal_values(key_list[5], (HEADS * HDIM, D), (HEADS * HDIM) ** -0.5, 0.09375, ((1, 8),))
    return dict(query_rows=query_rows, key_rows=key_rows, value_rows=value_rows, frequencies=frequencies, norm_gain=norm_gain, out_weight=out_weight)


def features_of(inputs, frequencies):
    phases = jnp.einsum('thd,hdf->thf', inputs.astype(jnp.float32), frequencies.astype(jnp.float32))
    joined = jnp.concatenate([jnp.cos(phases), jnp.sin(phases)], axis=-1)
    return (joined * (1.0 / math.sqrt(NFREQ))).astype(jnp.bfloat16)

def reference(query_rows, key_rows, value_rows, frequencies, norm_gain, out_weight):
    span_count = SEQ_LEN // BLOCK
    span_shape = (span_count, BLOCK, HEADS, HDIM)
    query_spans = query_rows.reshape(span_shape)
    key_spans = key_rows.reshape(span_shape)
    value_spans = value_rows.reshape(span_shape)
    gain_table = norm_gain.astype(jnp.float32).reshape(HEADS, HDIM)
    causal = jnp.arange(BLOCK)[:, None] >= jnp.arange(BLOCK)[None, :]

    def advance(running, pieces):
        query_part, key_part, value_part = pieces
        query_feat = features_of(query_part, frequencies).astype(jnp.float32)
        key_feat = features_of(key_part, frequencies).astype(jnp.float32)
        value_wide = value_part.astype(jnp.float32)
        carried_low = running.astype(jnp.bfloat16)
        scores = jnp.einsum('thf,shf->hts', query_feat, key_feat)
        scores = jnp.where(causal[None], scores, jnp.zeros_like(scores)).astype(jnp.bfloat16)
        local_part = jnp.einsum('hts,shd->thd', scores.astype(jnp.float32), value_wide)
        prior_part = jnp.einsum('thf,hfd->thd', query_feat, carried_low.astype(jnp.float32))
        attended = local_part + prior_part
        mean_square = lax.optimization_barrier(jnp.mean(attended * attended, axis=-1, keepdims=True))
        normed = (attended * lax.rsqrt(mean_square + 1e-06) * gain_table[None]).astype(jnp.bfloat16)
        projected_part = jnp.dot(normed.reshape(BLOCK, HEADS * HDIM), out_weight, preferred_element_type=jnp.float32).astype(jnp.bfloat16)
        updated = running + jnp.einsum('thf,thd->hfd', key_feat, value_wide)
        return (updated, projected_part)
    start_state = jnp.zeros((HEADS, FEATS, HDIM), jnp.float32)
    _, projected = lax.scan(advance, start_state, (query_spans, key_spans, value_spans))
    return projected.reshape(SEQ_LEN, D)
```

```python
import functools
import math

import jax
import jax.numpy as jnp
from jax import lax
from jax.experimental import pallas as pl
from jax.experimental.pallas import tpu as pltpu
from jax.sharding import PartitionSpec as P

MESH = pl.DeviceIdType.MESH
F32 = jnp.float32
BF16 = jnp.bfloat16
HEADS = 4
HDIM = 128
FEATS = 256
ROWS = 1024
BLOCK = 512
TILE = 256
PIECES = 4
RING = 8

TWO_PI_HIGH = 6.28125
TWO_PI_LOW = 2.0 * math.pi - TWO_PI_HIGH
ROUNDER = 12582912.0
SCALE = 1.0 / math.sqrt(128.0)


def half_angle_tables():
    import numpy as np

    root = math.sqrt(2.0 * SCALE)
    nodes = np.cos(np.pi * (np.arange(400) + 0.5) / 400.0) * np.pi**2 * 0.5 + np.pi**2 * 0.5
    angle = np.sqrt(nodes)
    cheb = np.polynomial.chebyshev.Chebyshev
    sine = cheb.fit(nodes, root * np.sin(angle / 2.0) / angle, 4, domain=[0.0, np.pi**2])
    cosine = cheb.fit(nodes, root * np.cos(angle / 2.0), 4, domain=[0.0, np.pi**2])
    poly = np.polynomial.Polynomial
    return (
        [float(v) for v in sine.convert(kind=poly, domain=[-1, 1]).coef],
        [float(v) for v in cosine.convert(kind=poly, domain=[-1, 1]).coef],
    )


SINE, COSINE = half_angle_tables()


def horner(z, table):
    out = z * table[-1] + table[-2]
    for value in table[-3::-1]:
        out = out * z + value
    return out


def cos_sin(phase):
    turns = (phase * (1.0 / (2.0 * math.pi)) + ROUNDER) - ROUNDER
    r = (phase - turns * TWO_PI_HIGH) - turns * TWO_PI_LOW
    z = r * r
    s = r * horner(z, SINE)
    c = horner(z, COSINE)
    return SCALE - s * s, s * c


def dot(a, b, dims=((1,), (0,))):
    return lax.dot_general(a, b, (dims, ((), ())), preferred_element_type=F32)


def columns(h):
    return pl.ds(pl.multiple_of(h * HDIM, HDIM), HDIM)


def tile_rows(p):
    return pl.ds(pl.multiple_of(p * TILE, TILE), TILE)


def kernel(
    q_hbm, k_hbm, v_hbm, freq_ref, gain_ref, w_hbm, out_hbm,
    q_ref, k_ref, v_ref, w_ref, qf, kf, state, local, full, acc, out_ref,
    swap_out, swap_in, first_out, first_in, second_out, second_in, give, take, carry, low,
    load_sem, store_sem, swap_sem, first_sem, second_sem, give_sem, ring_send, ring_recv,
):
    ctx = lax.axis_index("ctx")
    me = lax.axis_index("head")
    core = lax.rem(ctx, 2)
    x = lax.rem(ctx // 2, 4)
    y = ctx // 8
    right, left = lax.rem(me + 1, RING), lax.rem(me + RING - 1, RING)

    def at(y_, x_, core_):
        return (y_ * 4 + x_) * 2 + core_

    def along_x(i):
        return at(y, lax.rem(x + i, 4), core)

    def along_y(i):
        return at(lax.rem(y + i, 4), x, core)

    other = at(y, x, 1 - core)

    loads = [
        pltpu.make_async_copy(src, dst, load_sem.at[i])
        for i, (src, dst) in enumerate(
            ((k_hbm, k_ref), (v_hbm, v_ref), (q_hbm, q_ref), (w_hbm, w_ref))
        )
    ]
    for load in loads:
        load.start()

    barrier = pltpu.get_barrier_semaphore()

    def greet(c_, h_):
        pl.semaphore_signal(
            barrier, inc=1, device_id={"ctx": c_, "head": h_}, device_id_type=MESH
        )

    greet(other, me)
    for i in (1, 2, 3):
        greet(along_x(i), me)
        greet(along_y(i), me)
    greet(ctx, right)
    greet(ctx, left)

    def remote(src, dst, sems, slot, c_):
        return pltpu.make_async_remote_copy(
            src_ref=src, dst_ref=dst, send_sem=sems.at[0, slot], recv_sem=sems.at[1, slot],
            device_id={"ctx": c_, "head": me}, device_id_type=MESH,
        )

    def features(rows_ref, feat_ref, h):
        def chunk(p, _):
            phase = dot(rows_ref[tile_rows(p), columns(h)], freq_ref[h])
            cosine, sine = cos_sin(phase)
            feat_ref[h, tile_rows(p), 0:128] = cosine.astype(BF16)
            feat_ref[h, tile_rows(p), 128:256] = sine.astype(BF16)
            return 0

        lax.fori_loop(0, PIECES, chunk, 0)

    def key_side(j, _):
        h = lax.rem(j + 2 * (1 - core), HEADS)
        features(k_ref, kf, h)
        for b in (0, 1):
            rows = slice(b * BLOCK, (b + 1) * BLOCK)
            state[b, h] = dot(v_ref[rows, columns(h)], kf[h, rows, :], ((0,), (0,)))
        return 0

    loads[0].wait()
    loads[1].wait()
    lax.fori_loop(0, 2, key_side, 0)
    theirs = 2 * (1 - core)
    mine = 2 * core
    for j in (0, 1):
        swap_out[j] = (state[0, theirs + j] + state[1, theirs + j]).astype(BF16)
    pl.semaphore_wait(barrier, 9)
    swap = remote(swap_out, swap_in, swap_sem, 0, other)
    swap.start()
    lax.fori_loop(2, 4, key_side, 0)
    swap.wait()

    def own_total(j):
        return state[0, mine + j] + state[1, mine + j]

    for j in (0, 1):
        first_out[j] = (own_total(j) + swap_in[j].astype(F32)).astype(BF16)
    firsts = []
    for i in (2, 1, 3):
        peer = at(lax.rem(y + core * i, 4), lax.rem(x + (1 - core) * i, 4), core)
        firsts.append(remote(first_out, first_in.at[i - 1], first_sem, i - 1, peer))
        firsts[-1].start()

    loads[2].wait()

    def query_side(h, _):
        features(q_ref, qf, h)
        return 0

    lax.fori_loop(0, HEADS, query_side, 0)

    for copy in firsts:
        copy.wait()
    place = core * y + (1 - core) * x
    for j in (0, 1):
        chip = own_total(j) + swap_in[j].astype(F32)
        before = jnp.zeros_like(chip)
        line = chip
        for i in (1, 2, 3):
            piece = first_in[i - 1, j].astype(F32)
            line = line + piece
            before = before + jnp.where(place >= i, piece, 0.0)
        carry[j] = before
        through = before + chip
        for i in (1, 2, 3):
            column = jnp.where(x + i < 4, through, before)
            second_out[i - 1, j] = jnp.where(core == 0, line, column).astype(BF16)
    seconds = []
    for i in (2, 1, 3):
        peer = at(lax.rem(y + (1 - core) * i, 4), lax.rem(x + core * i, 4), core)
        seconds.append(
            remote(second_out.at[i - 1], second_in.at[i - 1], second_sem, i - 1, peer)
        )
        seconds[-1].start()

    causal = (
        lax.broadcasted_iota(jnp.int32, (TILE, TILE), 0)
        >= lax.broadcasted_iota(jnp.int32, (TILE, TILE), 1)
    )

    def attend(n, _):
        h, b = n // 2, lax.rem(n, 2)
        upper, lower = tile_rows(2 * b), tile_rows(2 * b + 1)

        def scores(rows, cols, masked):
            s = dot(qf[h, rows, :], kf[h, cols, :], ((1,), (1,)))
            return (jnp.where(causal, s, 0.0) if masked else s).astype(BF16)

        v0, v1 = v_ref[upper, columns(h)], v_ref[lower, columns(h)]
        local[upper, columns(h)] = dot(scores(upper, upper, True), v0)
        local[lower, columns(h)] = dot(scores(lower, upper, False), v0) + dot(
            scores(lower, lower, True), v1
        )
        return 0

    lax.fori_loop(0, 6, attend, 0)

    for copy in seconds:
        copy.wait()
    for j in (0, 1):
        total = carry[j]
        for i in (1, 2, 3):
            keep = core + jnp.where(y >= i, 1, 0) > 0
            total = total + jnp.where(keep, second_in[i - 1, j].astype(F32), 0.0)
        give[j] = (total + jnp.where(core == 0, own_total(j), 0.0)).astype(BF16)
        carry[j] = total + jnp.where(core == 1, swap_in[j].astype(F32), 0.0)
    hand = remote(give, take, give_sem, 0, other)
    hand.start()
    lax.fori_loop(6, 8, attend, 0)
    for j in (0, 1):
        low[0, mine + j] = carry[j].astype(BF16)
        low[1, mine + j] = (carry[j] + state[0, mine + j]).astype(BF16)
    hand.wait()
    for j in (0, 1):
        arrived = take[j].astype(F32)
        low[0, theirs + j] = arrived.astype(BF16)
        low[1, theirs + j] = (arrived + state[0, theirs + j]).astype(BF16)

    def hop(d, k, p):
        slot = lax.rem(me + RING - (k - 1), RING) if d == 0 else lax.rem(me + (k - 1), RING)
        piece = full.at[slot, tile_rows(p), :]
        return pltpu.make_async_remote_copy(
            src_ref=piece, dst_ref=piece,
            send_sem=ring_send.at[d, k - 1, p], recv_sem=ring_recv.at[d, k - 1, p],
            device_id={"ctx": ctx, "head": right if d == 0 else left}, device_id_type=MESH,
        )

    def project(slot, p, first=False):
        term = dot(
            full[slot, tile_rows(p), :], w_ref[pl.ds(pl.multiple_of(slot * 512, 512), 512), :]
        )
        if first:
            acc[tile_rows(p), :] = term
        else:
            acc[tile_rows(p), :] += term

    def finish(p, _):
        rows = tile_rows(p)
        for h in range(HEADS):
            cols = slice(h * HDIM, (h + 1) * HDIM)
            attended = local[rows, cols] + dot(
                qf[h, rows, :], low[p // 2, h], ((1,), (1,))
            )
            square = jnp.mean(attended * attended, axis=-1, keepdims=True)
            gain = gain_ref[0:1, cols].astype(F32)
            full[me, rows, cols] = (attended * lax.rsqrt(square + 1e-06) * gain).astype(BF16)
        hop(0, 1, p).start()
        hop(1, 1, p).start()
        return 0

    lax.fori_loop(0, PIECES, finish, 0)
    loads[3].wait()

    def own(p, _):
        project(me, p, True)
        return 0

    lax.fori_loop(0, PIECES, own, 0)

    def receive(n, _):
        k, p = n // PIECES + 1, lax.rem(n, PIECES)
        for d in (0, 1):
            hop(d, k, p).wait_recv()
            further = (k < 3) | ((p < 2) if d == 0 else (p >= 2))

            @pl.when(further)
            def _():
                hop(d, k + 1, p).start()

            slot = lax.rem(me + RING - k, RING) if d == 0 else lax.rem(me + k, RING)
            project(slot, p)
        return 0

    lax.fori_loop(0, 3 * PIECES, receive, 0)

    opposite = lax.rem(me + 4, RING)
    stores = []
    for p, d in ((0, 0), (2, 1), (1, 0), (3, 1)):
        hop(d, 4, p).wait_recv()
        project(opposite, p)
        out_ref[tile_rows(p), :] = acc[tile_rows(p), :].astype(BF16)
        stores.append(
            pltpu.make_async_copy(
                out_ref.at[tile_rows(p), :], out_hbm.at[tile_rows(p), :], store_sem.at[p]
            )
        )
        stores[-1].start()

    def drain(n, _):
        k, p = n // PIECES + 1, lax.rem(n, PIECES)
        for d in (0, 1):
            hop(d, k, p).wait_send()
        return 0

    lax.fori_loop(0, 3 * PIECES, drain, 0)
    for p, d in ((0, 0), (2, 1), (1, 0), (3, 1)):
        hop(d, 4, p).wait_send()
    for store in stores:
        store.wait()


def local(query_rows, key_rows, value_rows, frequencies, norm_gain, out_weight):
    anywhere = pl.BlockSpec(memory_space=pl.ANY)
    vmem = pl.BlockSpec(memory_space=pltpu.VMEM)
    pair = (2, HDIM, FEATS)
    return pl.pallas_call(
        kernel,
        out_shape=jax.ShapeDtypeStruct((ROWS, 512), BF16),
        in_specs=[anywhere, anywhere, anywhere, vmem, vmem, anywhere],
        out_specs=anywhere,
        scratch_shapes=[
            pltpu.VMEM((ROWS, 512), BF16),
            pltpu.VMEM((ROWS, 512), BF16),
            pltpu.VMEM((ROWS, 512), BF16),
            pltpu.VMEM((4096, 512), BF16),
            pltpu.VMEM((HEADS, ROWS, FEATS), BF16),
            pltpu.VMEM((HEADS, ROWS, FEATS), BF16),
            pltpu.VMEM((2, HEADS, HDIM, FEATS), F32),
            pltpu.VMEM((ROWS, 512), F32),
            pltpu.VMEM((RING, ROWS, 512), BF16),
            pltpu.VMEM((ROWS, 512), F32),
            pltpu.VMEM((ROWS, 512), BF16),
            pltpu.VMEM(pair, BF16),
            pltpu.VMEM(pair, BF16),
            pltpu.VMEM(pair, BF16),
            pltpu.VMEM((3,) + pair, BF16),
            pltpu.VMEM((3,) + pair, BF16),
            pltpu.VMEM((3,) + pair, BF16),
            pltpu.VMEM(pair, BF16),
            pltpu.VMEM(pair, BF16),
            pltpu.VMEM(pair, F32),
            pltpu.VMEM((2, HEADS, HDIM, FEATS), BF16),
            pltpu.SemaphoreType.DMA((4,)),
            pltpu.SemaphoreType.DMA((PIECES,)),
            pltpu.SemaphoreType.DMA((2, 1)),
            pltpu.SemaphoreType.DMA((2, 3)),
            pltpu.SemaphoreType.DMA((2, 3)),
            pltpu.SemaphoreType.DMA((2, 1)),
            pltpu.SemaphoreType.DMA((2, 4, PIECES)),
            pltpu.SemaphoreType.DMA((2, 4, PIECES)),
        ],
        compiler_params=pltpu.CompilerParams(
            collective_id=0, has_side_effects=True, vmem_limit_bytes=50 * 2**20
        ),
        cost_estimate=pl.CostEstimate(
            flops=7 * 10**9, bytes_accessed=9 * 2**20, transcendentals=0
        ),
    )(query_rows, key_rows, value_rows, frequencies, norm_gain.reshape(1, 512), out_weight)


def solution(mesh):
    return jax.shard_map(
        local,
        mesh=mesh,
        in_specs=(
            P("ctx", "head"),
            P("ctx", "head"),
            P("ctx", "head"),
            P("head", None, None),
            P("head"),
            P(None, "head"),
        ),
        out_specs=P("ctx", "head"),
        check_vma=False,
    )
```

```python
import functools
import math

import jax
import jax.numpy as jnp
from jax import lax
from jax.experimental import pallas as pl
from jax.experimental.pallas import tpu as pltpu
from jax.sharding import PartitionSpec as P

MESH = pl.DeviceIdType.MESH
F32 = jnp.float32
BF16 = jnp.bfloat16
HEADS = 4
HDIM = 128
FEATS = 256
ROWS = 1024
BLOCK = 512
TILE = 256
PIECES = 4
RING = 8
SLICE = 128

TWO_PI_HIGH = 6.28125
TWO_PI_LOW = 2.0 * math.pi - TWO_PI_HIGH
ROUNDER = 12582912.0
SCALE = 1.0 / math.sqrt(128.0)


def half_angle_tables():
    import numpy as np

    root = math.sqrt(2.0 * SCALE)
    nodes = np.cos(np.pi * (np.arange(400) + 0.5) / 400.0) * np.pi**2 * 0.5 + np.pi**2 * 0.5
    angle = np.sqrt(nodes)
    cheb = np.polynomial.chebyshev.Chebyshev
    sine = cheb.fit(nodes, root * np.sin(angle / 2.0) / angle, 4, domain=[0.0, np.pi**2])
    cosine = cheb.fit(nodes, root * np.cos(angle / 2.0), 4, domain=[0.0, np.pi**2])
    poly = np.polynomial.Polynomial
    return (
        [float(v) for v in sine.convert(kind=poly, domain=[-1, 1]).coef],
        [float(v) for v in cosine.convert(kind=poly, domain=[-1, 1]).coef],
    )


SINE, COSINE = half_angle_tables()


def horner(z, table):
    out = z * table[-1] + table[-2]
    for value in table[-3::-1]:
        out = out * z + value
    return out


def cos_sin(phase):
    turns = (phase * (1.0 / (2.0 * math.pi)) + ROUNDER) - ROUNDER
    r = (phase - turns * TWO_PI_HIGH) - turns * TWO_PI_LOW
    z = r * r
    s = r * horner(z, SINE)
    c = horner(z, COSINE)
    return SCALE - s * s, s * c


def dot(a, b, dims=((1,), (0,))):
    return lax.dot_general(a, b, (dims, ((), ())), preferred_element_type=F32)


def columns(h):
    return pl.ds(pl.multiple_of(h * HDIM, HDIM), HDIM)


def tile_rows(p):
    return pl.ds(pl.multiple_of(p * TILE, TILE), TILE)


def kernel(
    q_hbm, k_hbm, v_hbm, freq_ref, gain_ref, w_hbm, out_hbm,
    q_ref, k_ref, v_ref, w_ref, qf, kf, state, local, normed, full, acc, out_ref,
    swap_out, swap_in, first_out, first_in, second_out, second_in, give, take, carry, low,
    load_sem, swap_sem, first_sem, second_sem, give_sem,
    w_z_sem, w_first_sem, w_second_sem, w_core_sem, rows_sem, pass_sem, back_sem,
):
    ctx = lax.axis_index("ctx")
    me = lax.axis_index("head")
    core = lax.rem(ctx, 2)
    x = lax.rem(ctx // 2, 4)
    y = ctx // 8
    pair = me // 2
    sign = 1 - 2 * lax.rem(me, 2)
    mate = lax.rem(me + sign + RING, RING)

    def member(r):
        return 2 * r + lax.rem(me + pair // 2 + r // 2, 2)

    def at(y_, x_, core_):
        return (y_ * 4 + x_) * 2 + core_

    def along_x(i):
        return at(y, lax.rem(x + i, 4), core)

    def along_y(i):
        return at(lax.rem(y + i, 4), x, core)

    other = at(y, x, 1 - core)

    loads = [
        pltpu.make_async_copy(src, dst, load_sem.at[i])
        for i, (src, dst) in enumerate(
            ((k_hbm, k_ref), (v_hbm, v_ref), (q_hbm, q_ref), (w_hbm, w_ref.at[pair]))
        )
    ]
    for load in loads:
        load.start()

    barrier = pltpu.get_barrier_semaphore()

    def greet(c_, h_):
        pl.semaphore_signal(
            barrier, inc=1, device_id={"ctx": c_, "head": h_}, device_id_type=MESH
        )

    greet(other, me)
    for i in (1, 2, 3):
        greet(along_x(i), me)
        greet(along_y(i), me)
    for i in (1, 2, 3, 5, 6, 7):
        greet(ctx, lax.rem(me + i, RING))

    def remote(src, dst, sems, slot, c_):
        return pltpu.make_async_remote_copy(
            src_ref=src, dst_ref=dst, send_sem=sems.at[0, slot], recv_sem=sems.at[1, slot],
            device_id={"ctx": c_, "head": me}, device_id_type=MESH,
        )

    def remote_z(src, dst, sems, slot, h_):
        return pltpu.make_async_remote_copy(
            src_ref=src, dst_ref=dst, send_sem=sems.at[0, slot], recv_sem=sems.at[1, slot],
            device_id={"ctx": ctx, "head": h_}, device_id_type=MESH,
        )

    def first_peer(i):
        return at(lax.rem(y + core * i, 4), lax.rem(x + (1 - core) * i, 4), core)

    def second_peer(i):
        return at(lax.rem(y + (1 - core) * i, 4), lax.rem(x + core * i, 4), core)

    first_place = core * y + (1 - core) * x
    second_place = core * x + (1 - core) * y
    half_rows = core * 2048

    def slot_of(i):
        return lax.rem(pair + 4 - i, 4)

    def w_piece(i, start, size):
        return w_ref.at[slot_of(i), pl.ds(pl.multiple_of(start, SLICE), size), :]

    line_start = half_rows + second_place * 512
    slice_start = line_start + first_place * SLICE

    def w_z(i):
        rows = pl.ds(pl.multiple_of(slice_start, SLICE), SLICE)
        return remote_z(
            w_hbm.at[rows, :], w_ref.at[pair, rows, :], w_z_sem, i - 1, member(lax.rem(pair + i, 4))
        )

    def w_z_arrived(i):
        piece = w_piece(i, slice_start, SLICE)
        remote_z(piece, piece, w_z_sem, i - 1, member(slot_of(i))).wait_recv()

    def w_first(i, o):
        piece = w_piece(i, slice_start, SLICE)
        return remote(piece, piece, w_first_sem.at[i - 1], o - 1, first_peer(o))

    def w_first_arrived(i, o):
        piece = w_piece(i, line_start + lax.rem(first_place + 4 - o, 4) * SLICE, SLICE)
        remote(piece, piece, w_first_sem.at[i - 1], o - 1, first_peer(o)).wait_recv()

    def w_second(i, o):
        piece = w_piece(i, line_start, 512)
        return remote(piece, piece, w_second_sem.at[i - 1], o - 1, second_peer(o))

    def w_second_arrived(i, o):
        piece = w_piece(i, half_rows + lax.rem(second_place + 4 - o, 4) * 512, 512)
        remote(piece, piece, w_second_sem.at[i - 1], o - 1, second_peer(o)).wait_recv()

    def w_core(i):
        piece = w_piece(i, half_rows, 2048)
        return remote(piece, piece, w_core_sem, i - 1, other)

    def w_core_arrived(i):
        piece = w_piece(i, 2048 - half_rows, 2048)
        remote(piece, piece, w_core_sem, i - 1, other).wait_recv()

    def features(rows_ref, feat_ref, h):
        def chunk(p, _):
            phase = dot(rows_ref[tile_rows(p), columns(h)], freq_ref[h])
            cosine, sine = cos_sin(phase)
            feat_ref[h, tile_rows(p), 0:128] = cosine.astype(BF16)
            feat_ref[h, tile_rows(p), 128:256] = sine.astype(BF16)
            return 0

        lax.fori_loop(0, PIECES, chunk, 0)

    def key_side(j, _):
        h = lax.rem(j + 2 * (1 - core), HEADS)
        features(k_ref, kf, h)
        for b in (0, 1):
            rows = slice(b * BLOCK, (b + 1) * BLOCK)
            state[b, h] = dot(v_ref[rows, columns(h)], kf[h, rows, :], ((0,), (0,)))
        return 0

    loads[0].wait()
    loads[1].wait()
    lax.fori_loop(0, 2, key_side, 0)
    theirs = 2 * (1 - core)
    mine = 2 * core
    for j in (0, 1):
        swap_out[j] = (state[0, theirs + j] + state[1, theirs + j]).astype(BF16)
    pl.semaphore_wait(barrier, 13)
    swap = remote(swap_out, swap_in, swap_sem, 0, other)
    swap.start()
    for i in (1, 2, 3):
        w_z(i).start()
    lax.fori_loop(2, 4, key_side, 0)
    swap.wait()

    def own_total(j):
        return state[0, mine + j] + state[1, mine + j]

    for j in (0, 1):
        first_out[j] = (own_total(j) + swap_in[j].astype(F32)).astype(BF16)
    firsts = []
    for i in (2, 1, 3):
        firsts.append(
            remote(first_out, first_in.at[i - 1], first_sem, i - 1, first_peer(i))
        )
        firsts[-1].start()

    loads[2].wait()

    def query_side(h, _):
        features(q_ref, qf, h)
        return 0

    lax.fori_loop(0, HEADS, query_side, 0)

    for copy in firsts:
        copy.wait()
    for j in (0, 1):
        chip = own_total(j) + swap_in[j].astype(F32)
        before = jnp.zeros_like(chip)
        line = chip
        for i in (1, 2, 3):
            piece = first_in[i - 1, j].astype(F32)
            line = line + piece
            before = before + jnp.where(first_place >= i, piece, 0.0)
        carry[j] = before
        through = before + chip
        for i in (1, 2, 3):
            column = jnp.where(x + i < 4, through, before)
            second_out[i - 1, j] = jnp.where(core == 0, line, column).astype(BF16)
    seconds = []
    for i in (2, 1, 3):
        seconds.append(
            remote(second_out.at[i - 1], second_in.at[i - 1], second_sem, i - 1, second_peer(i))
        )
        seconds[-1].start()
    for i in (1, 2, 3):
        w_z_arrived(i)
        for o in (2, 1, 3):
            w_first(i, o).start()

    causal = (
        lax.broadcasted_iota(jnp.int32, (TILE, TILE), 0)
        >= lax.broadcasted_iota(jnp.int32, (TILE, TILE), 1)
    )

    def attend(n, _):
        h, b = n // 2, lax.rem(n, 2)
        upper, lower = tile_rows(2 * b), tile_rows(2 * b + 1)

        def scores(rows, cols, masked):
            s = dot(qf[h, rows, :], kf[h, cols, :], ((1,), (1,)))
            return (jnp.where(causal, s, 0.0) if masked else s).astype(BF16)

        v0, v1 = v_ref[upper, columns(h)], v_ref[lower, columns(h)]
        local[upper, columns(h)] = dot(scores(upper, upper, True), v0)
        local[lower, columns(h)] = dot(scores(lower, upper, False), v0) + dot(
            scores(lower, lower, True), v1
        )
        return 0

    lax.fori_loop(0, 6, attend, 0)

    for copy in seconds:
        copy.wait()
    for j in (0, 1):
        total = carry[j]
        for i in (1, 2, 3):
            keep = core + jnp.where(y >= i, 1, 0) > 0
            total = total + jnp.where(keep, second_in[i - 1, j].astype(F32), 0.0)
        give[j] = (total + jnp.where(core == 0, own_total(j), 0.0)).astype(BF16)
        carry[j] = total + jnp.where(core == 1, swap_in[j].astype(F32), 0.0)
    hand = remote(give, take, give_sem, 0, other)
    hand.start()
    lax.fori_loop(6, 8, attend, 0)
    for j in (0, 1):
        low[0, mine + j] = carry[j].astype(BF16)
        low[1, mine + j] = (carry[j] + state[0, mine + j]).astype(BF16)
    hand.wait()
    for j in (0, 1):
        arrived = take[j].astype(F32)
        low[0, theirs + j] = arrived.astype(BF16)
        low[1, theirs + j] = (arrived + state[0, theirs + j]).astype(BF16)

    def to_pair(k):
        target = mate if k == 0 else lax.rem(me + sign * {1: -1, 2: 2, 3: -3}[k] + RING, RING)
        piece = normed.at[tile_rows(target // 2), :]
        return remote_z(piece, full.at[me], rows_sem, k, target)

    def rows_arrived(k):
        slot = mate if k == 0 else lax.rem(me - sign * k + RING, RING)
        piece = full.at[slot]
        remote_z(piece, piece, rows_sem, k, slot).wait_recv()

    def pass_on(k):
        piece = full.at[lax.rem(me - sign * k + RING, RING)]
        return remote_z(piece, piece, pass_sem, k - 1, mate)

    def passed(k):
        piece = full.at[lax.rem(me + sign * (k + 1) + RING, RING)]
        remote_z(piece, piece, pass_sem, k - 1, mate).wait_recv()

    def finish(q):
        rows = tile_rows(q)
        for h in range(HEADS):
            cols = slice(h * HDIM, (h + 1) * HDIM)
            attended = local[rows, cols] + dot(
                qf[h, rows, :], low[q // 2, h], ((1,), (1,))
            )
            square = jnp.mean(attended * attended, axis=-1, keepdims=True)
            gain = gain_ref[0:1, cols].astype(F32)
            normed[rows, cols] = (attended * lax.rsqrt(square + 1e-06) * gain).astype(BF16)

    for k, step in ((3, 2), (2, sign), (1, -sign), (0, 0)):
        finish(lax.rem(pair + step + 4, 4))
        to_pair(k).start()
    full[me] = normed[tile_rows(pair), :]

    def line(i):
        for o in (1, 2, 3):
            w_first_arrived(i, o)
        for o in (2, 1, 3):
            w_second(i, o).start()

    def halves(i):
        for o in (1, 2, 3):
            w_second_arrived(i, o)
        w_core(i).start()

    line(1)
    for k in (1, 2):
        rows_arrived(k)
        pass_on(k).start()
    halves(1)
    line(2)
    rows_arrived(3)
    pass_on(3).start()
    halves(2)
    line(3)
    rows_arrived(0)
    for k in (1, 2, 3):
        passed(k)

    def project(slot, target):
        for s in (0, 2, 4, 6):
            term = dot(full[s], w_ref[slot, s * 512 : s * 512 + 512, :]) + dot(
                full[s + 1], w_ref[slot, s * 512 + 512 : s * 512 + 1024, :]
            )
            if s == 0:
                acc[...] = term
            elif s < 6:
                acc[...] += term
            else:
                out_ref[target] = (acc[...] + term).astype(BF16)

    def back(i):
        return remote_z(
            out_ref.at[i], out_hbm.at[tile_rows(pair), :], back_sem, i - 1, member(slot_of(i))
        )

    def back_arrived(i):
        r = lax.rem(pair + i, 4)
        remote_z(out_ref.at[i], out_hbm.at[tile_rows(r), :], back_sem, i - 1, member(r)).wait_recv()

    for i in (1, 2):
        w_core_arrived(i)
        project(slot_of(i), i)
        back(i).start()
    loads[3].wait()
    project(pair, 0)
    keep = pltpu.make_async_copy(out_ref.at[0], out_hbm.at[tile_rows(pair), :], load_sem.at[0])
    keep.start()
    halves(3)
    w_core_arrived(3)
    project(slot_of(3), 3)
    back(3).start()

    keep.wait()
    for i in (1, 2, 3):
        w_z(i).wait_send()
        w_core(i).wait_send()
        pass_on(i).wait_send()
        for o in (1, 2, 3):
            w_first(i, o).wait_send()
            w_second(i, o).wait_send()
    for k in (0, 1, 2, 3):
        to_pair(k).wait_send()
    for i in (1, 2, 3):
        back(i).wait_send()
        back_arrived(i)


def local(query_rows, key_rows, value_rows, frequencies, norm_gain, out_weight):
    anywhere = pl.BlockSpec(memory_space=pl.ANY)
    vmem = pl.BlockSpec(memory_space=pltpu.VMEM)
    pair = (2, HDIM, FEATS)
    return pl.pallas_call(
        kernel,
        out_shape=jax.ShapeDtypeStruct((ROWS, 512), BF16),
        in_specs=[anywhere, anywhere, anywhere, vmem, vmem, anywhere],
        out_specs=anywhere,
        scratch_shapes=[
            pltpu.VMEM((ROWS, 512), BF16),
            pltpu.VMEM((ROWS, 512), BF16),
            pltpu.VMEM((ROWS, 512), BF16),
            pltpu.VMEM((4, 4096, 512), BF16),
            pltpu.VMEM((HEADS, ROWS, FEATS), BF16),
            pltpu.VMEM((HEADS, ROWS, FEATS), BF16),
            pltpu.VMEM((2, HEADS, HDIM, FEATS), F32),
            pltpu.VMEM((ROWS, 512), F32),
            pltpu.VMEM((ROWS, 512), BF16),
            pltpu.VMEM((RING, TILE, 512), BF16),
            pltpu.VMEM((TILE, 512), F32),
            pltpu.VMEM((4, TILE, 512), BF16),
            pltpu.VMEM(pair, BF16),
            pltpu.VMEM(pair, BF16),
            pltpu.VMEM(pair, BF16),
            pltpu.VMEM((3,) + pair, BF16),
            pltpu.VMEM((3,) + pair, BF16),
            pltpu.VMEM((3,) + pair, BF16),
            pltpu.VMEM(pair, BF16),
            pltpu.VMEM(pair, BF16),
            pltpu.VMEM(pair, F32),
            pltpu.VMEM((2, HEADS, HDIM, FEATS), BF16),
            pltpu.SemaphoreType.DMA((4,)),
            pltpu.SemaphoreType.DMA((2, 1)),
            pltpu.SemaphoreType.DMA((2, 3)),
            pltpu.SemaphoreType.DMA((2, 3)),
            pltpu.SemaphoreType.DMA((2, 1)),
            pltpu.SemaphoreType.DMA((2, 3)),
            pltpu.SemaphoreType.DMA((3, 2, 3)),
            pltpu.SemaphoreType.DMA((3, 2, 3)),
            pltpu.SemaphoreType.DMA((2, 3)),
            pltpu.SemaphoreType.DMA((2, 4)),
            pltpu.SemaphoreType.DMA((2, 3)),
            pltpu.SemaphoreType.DMA((2, 3)),
        ],
        compiler_params=pltpu.CompilerParams(
            collective_id=0, has_side_effects=True, vmem_limit_bytes=63 * 2**20
        ),
        cost_estimate=pl.CostEstimate(
            flops=7 * 10**9, bytes_accessed=9 * 2**20, transcendentals=0
        ),
    )(query_rows, key_rows, value_rows, frequencies, norm_gain.reshape(1, 512), out_weight)


def solution(mesh):
    return jax.shard_map(
        local,
        mesh=mesh,
        in_specs=(
            P("ctx", "head"),
            P("ctx", "head"),
            P("ctx", "head"),
            P("head", None, None),
            P("head"),
            P(None, "head"),
        ),
        out_specs=P("ctx", "head"),
        check_vma=False,
    )
```

```python
import functools
import math

import jax
import jax.numpy as jnp
from jax import lax
from jax.experimental import pallas as pl
from jax.experimental.pallas import tpu as pltpu
from jax.sharding import PartitionSpec as P

MESH = pl.DeviceIdType.MESH
F32 = jnp.float32
BF16 = jnp.bfloat16
HEADS = 4
HDIM = 128
FEATS = 256
ROWS = 1024
BLOCK = 512
TILE = 256
PIECES = 4
RING = 8
SLICE = 128
SEATS = 8
PART = 64
HALF = 128

TWO_PI_HIGH = 6.28125
TWO_PI_LOW = 2.0 * math.pi - TWO_PI_HIGH
ROUNDER = 12582912.0
SCALE = 1.0 / math.sqrt(128.0)


def half_angle_tables():
    import numpy as np

    root = math.sqrt(2.0 * SCALE)
    nodes = np.cos(np.pi * (np.arange(400) + 0.5) / 400.0) * np.pi**2 * 0.5 + np.pi**2 * 0.5
    angle = np.sqrt(nodes)
    cheb = np.polynomial.chebyshev.Chebyshev
    sine = cheb.fit(nodes, root * np.sin(angle / 2.0) / angle, 4, domain=[0.0, np.pi**2])
    cosine = cheb.fit(nodes, root * np.cos(angle / 2.0), 4, domain=[0.0, np.pi**2])
    poly = np.polynomial.Polynomial
    return (
        [float(v) for v in sine.convert(kind=poly, domain=[-1, 1]).coef],
        [float(v) for v in cosine.convert(kind=poly, domain=[-1, 1]).coef],
    )


SINE, COSINE = half_angle_tables()


def horner(z, table):
    out = z * table[-1] + table[-2]
    for value in table[-3::-1]:
        out = out * z + value
    return out


def cos_sin(phase):
    turns = (phase * (1.0 / (2.0 * math.pi)) + ROUNDER) - ROUNDER
    r = (phase - turns * TWO_PI_HIGH) - turns * TWO_PI_LOW
    z = r * r
    s = r * horner(z, SINE)
    c = horner(z, COSINE)
    return SCALE - s * s, s * c


def dot(a, b, dims=((1,), (0,))):
    return lax.dot_general(a, b, (dims, ((), ())), preferred_element_type=F32)


def columns(h):
    return pl.ds(pl.multiple_of(h * HDIM, HDIM), HDIM)


def tile_rows(p):
    return pl.ds(pl.multiple_of(p * TILE, TILE), TILE)


def kernel(
    q_hbm, k_hbm, v_hbm, freq_hbm, gain_hbm, w_hbm, out_hbm,
    q_ref, k_ref, v_ref, freq_ref, gain_ref, w_ref, qf, kf, state, local, normed, full, acc, out_ref,
    total, parts, row_out, row_in, sums, low,
    load_sem, parts_sem, row_sem, sums_sem,
    w_z_sem, w_first_sem, w_second_sem, w_core_sem, rows_sem, pass_sem, back_sem,
):
    ctx = lax.axis_index("ctx")
    me = lax.axis_index("head")
    core = lax.rem(ctx, 2)
    x = lax.rem(ctx // 2, 4)
    y = ctx // 8
    pair = me // 2
    sign = 1 - 2 * lax.rem(me, 2)
    mate = lax.rem(me + sign + RING, RING)

    def member(r):
        return 2 * r + lax.rem(me + pair // 2 + r // 2, 2)

    def at(y_, x_, core_):
        return (y_ * 4 + x_) * 2 + core_

    def row_seat(i):
        return y * SEATS + lax.rem(i, SEATS)

    def along_y(i):
        return at(lax.rem(y + i, 4), x, core)

    other = at(y, x, 1 - core)
    seat = 2 * x + core

    loads = [
        pltpu.make_async_copy(src, dst, load_sem.at[i])
        for i, (src, dst) in enumerate(
            (
                (freq_hbm, freq_ref), (k_hbm, k_ref), (v_hbm, v_ref), (q_hbm, q_ref),
                (gain_hbm, gain_ref), (w_hbm, w_ref.at[pair]),
            )
        )
    ]
    for load in loads:
        load.start()

    barrier = pltpu.get_barrier_semaphore()

    def greet(c_, h_):
        pl.semaphore_signal(
            barrier, inc=1, device_id={"ctx": c_, "head": h_}, device_id_type=MESH
        )

    for i in range(1, SEATS):
        greet(row_seat(seat + i), me)
    for i in (1, 2, 3):
        greet(along_y(i), me)
    for i in (1, 2, 3, 5, 6, 7):
        greet(ctx, lax.rem(me + i, RING))

    def remote(src, dst, sems, slot, c_):
        return pltpu.make_async_remote_copy(
            src_ref=src, dst_ref=dst, send_sem=sems.at[0, slot], recv_sem=sems.at[1, slot],
            device_id={"ctx": c_, "head": me}, device_id_type=MESH,
        )

    def remote_z(src, dst, sems, slot, h_):
        return pltpu.make_async_remote_copy(
            src_ref=src, dst_ref=dst, send_sem=sems.at[0, slot], recv_sem=sems.at[1, slot],
            device_id={"ctx": ctx, "head": h_}, device_id_type=MESH,
        )

    def first_peer(i):
        return at(lax.rem(y + core * i, 4), lax.rem(x + (1 - core) * i, 4), core)

    def second_peer(i):
        return at(lax.rem(y + (1 - core) * i, 4), lax.rem(x + core * i, 4), core)

    first_place = core * y + (1 - core) * x
    second_place = core * x + (1 - core) * y
    half_rows = core * 2048

    def slot_of(i):
        return lax.rem(pair + 4 - i, 4)

    def w_piece(i, start, size):
        return w_ref.at[slot_of(i), pl.ds(pl.multiple_of(start, SLICE), size), :]

    line_start = half_rows + second_place * 512
    slice_start = line_start + first_place * SLICE

    def w_z(i):
        rows = pl.ds(pl.multiple_of(slice_start, SLICE), SLICE)
        return remote_z(
            w_hbm.at[rows, :], w_ref.at[pair, rows, :], w_z_sem, i - 1, member(lax.rem(pair + i, 4))
        )

    def w_z_arrived(i):
        piece = w_piece(i, slice_start, SLICE)
        remote_z(piece, piece, w_z_sem, i - 1, member(slot_of(i))).wait_recv()

    def w_first(i, o):
        piece = w_piece(i, slice_start, SLICE)
        return remote(piece, piece, w_first_sem.at[i - 1], o - 1, first_peer(o))

    def w_first_arrived(i, o):
        piece = w_piece(i, line_start + lax.rem(first_place + 4 - o, 4) * SLICE, SLICE)
        remote(piece, piece, w_first_sem.at[i - 1], o - 1, first_peer(o)).wait_recv()

    def w_second(i, o):
        piece = w_piece(i, line_start, 512)
        return remote(piece, piece, w_second_sem.at[i - 1], o - 1, second_peer(o))

    def w_second_arrived(i, o):
        piece = w_piece(i, half_rows + lax.rem(second_place + 4 - o, 4) * 512, 512)
        remote(piece, piece, w_second_sem.at[i - 1], o - 1, second_peer(o)).wait_recv()

    def w_core(i):
        piece = w_piece(i, half_rows, 2048)
        return remote(piece, piece, w_core_sem, i - 1, other)

    def w_core_arrived(i):
        piece = w_piece(i, 2048 - half_rows, 2048)
        remote(piece, piece, w_core_sem, i - 1, other).wait_recv()

    def features(rows_ref, feat_ref, h):
        def chunk(p, _):
            phase = dot(rows_ref[tile_rows(p), columns(h)], freq_ref[h])
            cosine, sine = cos_sin(phase)
            feat_ref[h, tile_rows(p), 0:128] = cosine.astype(BF16)
            feat_ref[h, tile_rows(p), 128:256] = sine.astype(BF16)
            return 0

        lax.fori_loop(0, PIECES, chunk, 0)

    def head_rows(h):
        return pl.ds(pl.multiple_of(h * HDIM, HDIM), HDIM)

    def part(i):
        return pl.ds(pl.multiple_of(i * PART, PART), PART)

    def key_side(h, _):
        features(k_ref, kf, h)
        for b in (0, 1):
            rows = slice(b * BLOCK, (b + 1) * BLOCK)
            state[b, head_rows(h), :] = dot(v_ref[rows, columns(h)], kf[h, rows, :], ((0,), (0,)))
        total[head_rows(h), :] = (state[0, head_rows(h), :] + state[1, head_rows(h), :]).astype(BF16)
        return 0

    def send_part(i):
        return pltpu.make_async_remote_copy(
            src_ref=total.at[part(i), :], dst_ref=parts.at[seat],
            send_sem=parts_sem.at[0, i], recv_sem=parts_sem.at[1, seat],
            device_id={"ctx": row_seat(i), "head": me}, device_id_type=MESH,
        )

    def part_arrived(i):
        i = lax.rem(seat + i, SEATS)
        pltpu.make_async_remote_copy(
            src_ref=parts.at[i], dst_ref=parts.at[i],
            send_sem=parts_sem.at[0, i], recv_sem=parts_sem.at[1, i],
            device_id={"ctx": row_seat(i), "head": me}, device_id_type=MESH,
        ).wait_recv()

    def send_sum(i):
        return pltpu.make_async_remote_copy(
            src_ref=sums.at[i], dst_ref=low.at[0, part(seat), :],
            send_sem=sums_sem.at[0, i], recv_sem=sums_sem.at[1, seat],
            device_id={"ctx": row_seat(i), "head": me}, device_id_type=MESH,
        )

    def sum_arrived(i):
        i = lax.rem(seat + i, SEATS)
        piece = low.at[0, part(i), :]
        pltpu.make_async_remote_copy(
            src_ref=piece, dst_ref=piece,
            send_sem=sums_sem.at[0, i], recv_sem=sums_sem.at[1, i],
            device_id={"ctx": row_seat(i), "head": me}, device_id_type=MESH,
        ).wait_recv()

    def to_others(start, first, last):
        def step(i, _):
            @pl.when(i != seat)
            def _():
                start(i)

            return 0

        lax.fori_loop(first, last, step, 0)

    for load in loads[:3]:
        load.wait()
    lax.fori_loop(0, 2, key_side, 0)
    pl.semaphore_wait(barrier, 16)
    to_others(lambda i: send_part(i).start(), 0, 4)
    lax.fori_loop(2, 4, key_side, 0)
    to_others(lambda i: send_part(i).start(), 4, 8)
    for i in (1, 2, 3):
        w_z(i).start()
    parts[seat] = total[part(seat), :]

    loads[3].wait()
    loads[4].wait()

    def query_side(h, _):
        features(q_ref, qf, h)
        return 0

    lax.fori_loop(0, HEADS, query_side, 0)

    for i in range(1, SEATS):
        part_arrived(i)
    row_total = parts[0].astype(F32)
    for i in range(1, SEATS):
        row_total = row_total + parts[i].astype(F32)
    row_out[...] = row_total.astype(BF16)

    def send_row(i):
        return remote(row_out, row_in.at[i - 1], row_sem, i - 1, along_y(i))

    for i in (2, 1, 3):
        send_row(i).start()

    causal = (
        lax.broadcasted_iota(jnp.int32, (TILE, TILE), 0)
        >= lax.broadcasted_iota(jnp.int32, (TILE, TILE), 1)
    )

    def attend(n, _):
        h, b = n // 2, lax.rem(n, 2)
        upper, lower = tile_rows(2 * b), tile_rows(2 * b + 1)

        def scores(rows, cols, masked):
            s = dot(qf[h, rows, :], kf[h, cols, :], ((1,), (1,)))
            return (jnp.where(causal, s, 0.0) if masked else s).astype(BF16)

        v0, v1 = v_ref[upper, columns(h)], v_ref[lower, columns(h)]
        local[upper, columns(h)] = dot(scores(upper, upper, True), v0)
        local[lower, columns(h)] = dot(scores(lower, upper, False), v0) + dot(
            scores(lower, lower, True), v1
        )
        return 0

    lax.fori_loop(0, 3, attend, 0)

    for i in (1, 2, 3):
        send_row(i).wait()
    running = jnp.zeros((PART, FEATS), F32)
    for i in (1, 2, 3):
        running = running + jnp.where(y >= i, row_in[i - 1].astype(F32), 0.0)
    for i in range(SEATS):
        sums[i] = running.astype(BF16)
        if i < SEATS - 1:
            running = running + parts[i].astype(F32)
    to_others(lambda i: send_sum(i).start(), 0, 8)
    low[0, part(seat), :] = sums[seat]
    for i in (1, 2, 3):
        w_z_arrived(i)
        for o in (2, 1, 3):
            w_first(i, o).start()
    lax.fori_loop(3, 8, attend, 0)
    for i in range(1, SEATS):
        sum_arrived(i)
    low[1] = (low[0].astype(F32) + state[0]).astype(BF16)

    def half(q, t):
        return pl.ds(pl.multiple_of(q * TILE + t * HALF, HALF), HALF)

    def stored(slot, t):
        return full.at[lax.rem(slot + RING, RING), t * HALF : (t + 1) * HALF, :]

    def to_pair(t, k):
        target = mate if k == 0 else lax.rem(me + sign * {1: -1, 2: 2, 3: -3}[k] + RING, RING)
        piece = normed.at[half(target // 2, t), :]
        return remote_z(piece, stored(me, t), rows_sem.at[t], k, target)

    def rows_arrived(t, k):
        piece = stored(mate if k == 0 else me - sign * k, t)
        remote_z(piece, piece, rows_sem.at[t], k, mate).wait_recv()

    def pass_on(t, k):
        piece = stored(me - sign * k, t)
        return remote_z(piece, piece, pass_sem.at[t], k - 1, mate)

    def forward(t, k):
        rows_arrived(t, k)
        pass_on(t, k).start()

    def passed(t):
        for k in (1, 2, 3):
            piece = stored(me + sign * (k + 1), t)
            remote_z(piece, piece, pass_sem.at[t], k - 1, mate).wait_recv()

    def finish(q):
        rows = tile_rows(q)
        for h in range(HEADS):
            cols = slice(h * HDIM, (h + 1) * HDIM)
            attended = local[rows, cols] + dot(
                qf[h, rows, :], low[q // 2, h * HDIM : (h + 1) * HDIM, :], ((1,), (1,))
            )
            square = jnp.mean(attended * attended, axis=-1, keepdims=True)
            gain = gain_ref[cols].astype(F32).reshape(1, HDIM)
            normed[rows, cols] = (attended * lax.rsqrt(square + 1e-06) * gain).astype(BF16)

    def line(i):
        for o in (1, 2, 3):
            w_first_arrived(i, o)
        for o in (2, 1, 3):
            w_second(i, o).start()

    def halves(i):
        for o in (1, 2, 3):
            w_second_arrived(i, o)
        w_core(i).start()

    def project(slot, target, t):
        rows = slice(t * HALF, (t + 1) * HALF)
        for s in (0, 2, 4, 6):
            term = dot(full[s, rows, :], w_ref[slot, s * 512 : s * 512 + 512, :]) + dot(
                full[s + 1, rows, :], w_ref[slot, s * 512 + 512 : s * 512 + 1024, :]
            )
            if s == 0:
                acc[...] = term
            elif s < 6:
                acc[...] += term
            else:
                out_ref[target, rows, :] = (acc[...] + term).astype(BF16)

    def back(t, i):
        return remote_z(
            out_ref.at[i, t * HALF : (t + 1) * HALF, :], out_hbm.at[half(pair, t), :],
            back_sem.at[t], i - 1, member(slot_of(i)),
        )

    def back_arrived(t, i):
        r = lax.rem(pair + i, 4)
        piece = out_hbm.at[half(r, t), :]
        remote_z(
            out_ref.at[i, t * HALF : (t + 1) * HALF, :], piece, back_sem.at[t], i - 1, member(r)
        ).wait_recv()

    def give_back(t, i):
        project(slot_of(i), i, t)
        back(t, i).start()

    line(1)
    for k, step in ((3, 2), (2, sign), (1, -sign), (0, 0)):
        finish(lax.rem(pair + step + 4, 4))
        to_pair(0, k).start()
    to_pair(1, 0).start()
    full[me] = normed[tile_rows(pair), :]

    forward(0, 1)
    forward(0, 2)
    line(2)
    line(3)
    forward(0, 3)
    for k in (3, 2, 1):
        to_pair(1, k).start()
    rows_arrived(0, 0)
    halves(1)
    passed(0)
    w_core_arrived(1)
    give_back(0, 1)
    forward(1, 1)
    halves(2)
    w_core_arrived(2)
    give_back(0, 2)
    forward(1, 2)
    loads[5].wait()
    project(pair, 0, 0)
    forward(1, 3)
    halves(3)
    rows_arrived(1, 0)
    w_core_arrived(3)
    give_back(0, 3)
    passed(1)
    for i in (1, 2, 3):
        give_back(1, i)
    project(pair, 0, 1)
    keep = pltpu.make_async_copy(out_ref.at[0], out_hbm.at[tile_rows(pair), :], load_sem.at[0])
    keep.start()

    for i in (1, 2, 3):
        w_z(i).wait_send()
        w_core(i).wait_send()
        for o in (1, 2, 3):
            w_first(i, o).wait_send()
            w_second(i, o).wait_send()
    for t in (0, 1):
        for k in (1, 2, 3):
            pass_on(t, k).wait_send()
        for k in (0, 1, 2, 3):
            to_pair(t, k).wait_send()
    to_others(lambda i: send_part(i).wait_send(), 0, 8)
    to_others(lambda i: send_sum(i).wait_send(), 0, 8)
    keep.wait()
    for t in (0, 1):
        for i in (1, 2, 3):
            back(t, i).wait_send()
            back_arrived(t, i)


def local(query_rows, key_rows, value_rows, frequencies, norm_gain, out_weight):
    anywhere = pl.BlockSpec(memory_space=pl.ANY)
    operands = [
        pltpu.with_memory_space_constraint(operand, pltpu.HBM)
        for operand in (query_rows, key_rows, value_rows, frequencies, norm_gain, out_weight)
    ]
    return pl.pallas_call(
        kernel,
        out_shape=jax.ShapeDtypeStruct((ROWS, 512), BF16),
        in_specs=[anywhere] * 6,
        out_specs=anywhere,
        scratch_shapes=[
            pltpu.VMEM((ROWS, 512), BF16),
            pltpu.VMEM((ROWS, 512), BF16),
            pltpu.VMEM((ROWS, 512), BF16),
            pltpu.VMEM((HEADS, HDIM, HDIM), BF16),
            pltpu.VMEM((512,), BF16),
            pltpu.VMEM((4, 4096, 512), BF16),
            pltpu.VMEM((HEADS, ROWS, FEATS), BF16),
            pltpu.VMEM((HEADS, ROWS, FEATS), BF16),
            pltpu.VMEM((2, 512, FEATS), F32),
            pltpu.VMEM((ROWS, 512), F32),
            pltpu.VMEM((ROWS, 512), BF16),
            pltpu.VMEM((RING, TILE, 512), BF16),
            pltpu.VMEM((HALF, 512), F32),
            pltpu.VMEM((4, TILE, 512), BF16),
            pltpu.VMEM((512, FEATS), BF16),
            pltpu.VMEM((SEATS, PART, FEATS), BF16),
            pltpu.VMEM((PART, FEATS), BF16),
            pltpu.VMEM((3, PART, FEATS), BF16),
            pltpu.VMEM((SEATS, PART, FEATS), BF16),
            pltpu.VMEM((2, 512, FEATS), BF16),
            pltpu.SemaphoreType.DMA((6,)),
            pltpu.SemaphoreType.DMA((2, SEATS)),
            pltpu.SemaphoreType.DMA((2, 3)),
            pltpu.SemaphoreType.DMA((2, SEATS)),
            pltpu.SemaphoreType.DMA((2, 3)),
            pltpu.SemaphoreType.DMA((3, 2, 3)),
            pltpu.SemaphoreType.DMA((3, 2, 3)),
            pltpu.SemaphoreType.DMA((2, 3)),
            pltpu.SemaphoreType.DMA((2, 2, 4)),
            pltpu.SemaphoreType.DMA((2, 2, 3)),
            pltpu.SemaphoreType.DMA((2, 2, 3)),
        ],
        compiler_params=pltpu.CompilerParams(
            collective_id=0, has_side_effects=True, vmem_limit_bytes=50 * 2**20
        ),
        cost_estimate=pl.CostEstimate(
            flops=7 * 10**9, bytes_accessed=9 * 2**20, transcendentals=0
        ),
    )(*operands)


def solution(mesh):
    return jax.shard_map(
        local,
        mesh=mesh,
        in_specs=(
            P("ctx", "head"),
            P("ctx", "head"),
            P("ctx", "head"),
            P("head", None, None),
            P("head"),
            P(None, "head"),
        ),
        out_specs=P("ctx", "head"),
        check_vma=False,
    )
```

```python
import functools
import math

import jax
import jax.numpy as jnp
from jax import lax
from jax.experimental import pallas as pl
from jax.experimental.pallas import tpu as pltpu
from jax.sharding import PartitionSpec as P

MESH = pl.DeviceIdType.MESH
F32 = jnp.float32
BF16 = jnp.bfloat16
HEADS = 4
HDIM = 128
FEATS = 256
ROWS = 1024
BLOCK = 512
TILE = 256
PIECES = 4
RING = 8
SLICE = 128
SEATS = 8
PART = 64
HALF = 128

TWO_PI_HIGH = 6.28125
TWO_PI_LOW = 2.0 * math.pi - TWO_PI_HIGH
ROUNDER = 12582912.0
SCALE = 1.0 / math.sqrt(128.0)


def half_angle_tables():
    import numpy as np

    root = math.sqrt(2.0 * SCALE)
    nodes = np.cos(np.pi * (np.arange(400) + 0.5) / 400.0) * np.pi**2 * 0.5 + np.pi**2 * 0.5
    angle = np.sqrt(nodes)
    cheb = np.polynomial.chebyshev.Chebyshev
    sine = cheb.fit(nodes, root * np.sin(angle / 2.0) / angle, 4, domain=[0.0, np.pi**2])
    cosine = cheb.fit(nodes, root * np.cos(angle / 2.0), 4, domain=[0.0, np.pi**2])
    poly = np.polynomial.Polynomial
    return (
        [float(v) for v in sine.convert(kind=poly, domain=[-1, 1]).coef],
        [float(v) for v in cosine.convert(kind=poly, domain=[-1, 1]).coef],
    )


SINE, COSINE = half_angle_tables()


def horner(z, table):
    out = z * table[-1] + table[-2]
    for value in table[-3::-1]:
        out = out * z + value
    return out


def cos_sin(phase):
    turns = (phase * (1.0 / (2.0 * math.pi)) + ROUNDER) - ROUNDER
    r = (phase - turns * TWO_PI_HIGH) - turns * TWO_PI_LOW
    z = r * r
    s = r * horner(z, SINE)
    c = horner(z, COSINE)
    return SCALE - s * s, s * c


def dot(a, b, dims=((1,), (0,))):
    return lax.dot_general(a, b, (dims, ((), ())), preferred_element_type=F32)


def columns(h):
    return pl.ds(pl.multiple_of(h * HDIM, HDIM), HDIM)


def tile_rows(p):
    return pl.ds(pl.multiple_of(p * TILE, TILE), TILE)


def kernel(
    q_hbm, k_hbm, v_hbm, freq_hbm, gain_hbm, w_hbm, out_hbm,
    q_ref, k_ref, v_ref, freq_ref, gain_ref, w_ref, qf, kf, state, local, normed, full, acc, out_ref,
    total, parts, row_out, row_in, sums, low,
    load_sem, parts_sem, row_sem, sums_sem,
    w_z_sem, w_first_sem, w_second_sem, w_relay_sem, w_core_sem, rows_sem, pass_sem, back_sem,
):
    ctx = lax.axis_index("ctx")
    me = lax.axis_index("head")
    core = lax.rem(ctx, 2)
    x = lax.rem(ctx // 2, 4)
    y = ctx // 8
    pair = me // 2
    sign = 1 - 2 * lax.rem(me, 2)
    mate = lax.rem(me + sign + RING, RING)

    def member(r):
        return 2 * r + lax.rem(me + pair // 2 + r // 2, 2)

    def at(y_, x_, core_):
        return (y_ * 4 + x_) * 2 + core_

    def row_seat(i):
        return y * SEATS + lax.rem(i, SEATS)

    def along_y(i):
        return at(lax.rem(y + i, 4), x, core)

    other = at(y, x, 1 - core)
    seat = 2 * x + core

    loads = [
        pltpu.make_async_copy(src, dst, load_sem.at[i])
        for i, (src, dst) in enumerate(
            (
                (freq_hbm, freq_ref), (k_hbm, k_ref), (v_hbm, v_ref), (q_hbm, q_ref),
                (gain_hbm, gain_ref), (w_hbm, w_ref.at[pair]),
            )
        )
    ]
    for load in loads:
        load.start()

    barrier = pltpu.get_barrier_semaphore()

    def greet(c_, h_):
        pl.semaphore_signal(
            barrier, inc=1, device_id={"ctx": c_, "head": h_}, device_id_type=MESH
        )

    for i in range(1, SEATS):
        greet(row_seat(seat + i), me)
    for i in (1, 2, 3):
        greet(along_y(i), me)
    for i in (1, 2, 3, 5, 6, 7):
        greet(ctx, lax.rem(me + i, RING))

    def remote(src, dst, sems, slot, c_):
        return pltpu.make_async_remote_copy(
            src_ref=src, dst_ref=dst, send_sem=sems.at[0, slot], recv_sem=sems.at[1, slot],
            device_id={"ctx": c_, "head": me}, device_id_type=MESH,
        )

    def remote_z(src, dst, sems, slot, h_):
        return pltpu.make_async_remote_copy(
            src_ref=src, dst_ref=dst, send_sem=sems.at[0, slot], recv_sem=sems.at[1, slot],
            device_id={"ctx": ctx, "head": h_}, device_id_type=MESH,
        )

    def first_peer(i):
        return at(lax.rem(y + core * i, 4), lax.rem(x + (1 - core) * i, 4), core)

    def second_peer(i):
        return at(lax.rem(y + (1 - core) * i, 4), lax.rem(x + core * i, 4), core)

    first_place = core * y + (1 - core) * x
    second_place = core * x + (1 - core) * y
    half_rows = core * 2048

    def slot_of(i):
        return lax.rem(pair + 4 - i, 4)

    def w_piece(i, start, size):
        return w_ref.at[slot_of(i), pl.ds(pl.multiple_of(start, SLICE), size), :]

    line_start = half_rows + second_place * 512
    slice_start = line_start + first_place * SLICE

    def w_z(i):
        rows = pl.ds(pl.multiple_of(slice_start, SLICE), SLICE)
        return remote_z(
            w_hbm.at[rows, :], w_ref.at[pair, rows, :], w_z_sem, i - 1, member(lax.rem(pair + i, 4))
        )

    def w_z_arrived(i):
        piece = w_piece(i, slice_start, SLICE)
        remote_z(piece, piece, w_z_sem, i - 1, member(slot_of(i))).wait_recv()

    def w_first(i, o):
        piece = w_piece(i, slice_start, SLICE)
        return remote(piece, piece, w_first_sem.at[i - 1], o - 1, first_peer(o))

    def w_first_arrived(i, o):
        piece = w_piece(i, line_start + lax.rem(first_place + 4 - o, 4) * SLICE, SLICE)
        remote(piece, piece, w_first_sem.at[i - 1], o - 1, first_peer(o)).wait_recv()

    def w_second(i, o):
        piece = w_piece(i, line_start, 512)
        return remote(piece, piece, w_second_sem.at[i - 1], o - 1, second_peer(o))

    def w_second_arrived(i, o):
        piece = w_piece(i, half_rows + lax.rem(second_place + 4 - o, 4) * 512, 512)
        remote(piece, piece, w_second_sem.at[i - 1], o - 1, second_peer(o)).wait_recv()

    def w_relay(i, d):
        source = lax.rem(second_place + (3 if d == 0 else 1), 4)
        piece = w_piece(i, half_rows + source * 512 + d * 256, 256)
        return remote(piece, piece, w_relay_sem.at[i - 1], d, second_peer(1 if d == 0 else 3))

    def w_relay_arrived(i, d):
        piece = w_piece(i, half_rows + lax.rem(second_place + 2, 4) * 512 + d * 256, 256)
        remote(piece, piece, w_relay_sem.at[i - 1], d, second_peer(1)).wait_recv()

    def w_core(i, o):
        piece = w_piece(i, half_rows + lax.rem(second_place + 4 - o, 4) * 512, 512)
        return remote(piece, piece, w_core_sem.at[i - 1], o, other)

    def w_core_arrived(i):
        for o in (0, 1, 2, 3):
            piece = w_piece(i, 2048 - half_rows + o * 512, 512)
            remote(piece, piece, w_core_sem.at[i - 1], o, other).wait_recv()

    def features(rows_ref, feat_ref, h):
        def chunk(p, _):
            phase = dot(rows_ref[tile_rows(p), columns(h)], freq_ref[h])
            cosine, sine = cos_sin(phase)
            feat_ref[h, tile_rows(p), 0:128] = cosine.astype(BF16)
            feat_ref[h, tile_rows(p), 128:256] = sine.astype(BF16)
            return 0

        lax.fori_loop(0, PIECES, chunk, 0, unroll=True)

    def head_rows(h):
        return pl.ds(pl.multiple_of(h * HDIM, HDIM), HDIM)

    def part(i):
        return pl.ds(pl.multiple_of(i * PART, PART), PART)

    def key_side(h, _):
        features(k_ref, kf, h)
        for b in (0, 1):
            rows = slice(b * BLOCK, (b + 1) * BLOCK)
            state[b, head_rows(h), :] = dot(v_ref[rows, columns(h)], kf[h, rows, :], ((0,), (0,)))
        total[head_rows(h), :] = (state[0, head_rows(h), :] + state[1, head_rows(h), :]).astype(BF16)
        return 0

    def send_part(i):
        return pltpu.make_async_remote_copy(
            src_ref=total.at[part(i), :], dst_ref=parts.at[seat],
            send_sem=parts_sem.at[0, i], recv_sem=parts_sem.at[1, seat],
            device_id={"ctx": row_seat(i), "head": me}, device_id_type=MESH,
        )

    def part_arrived(i):
        i = lax.rem(seat + i, SEATS)
        pltpu.make_async_remote_copy(
            src_ref=parts.at[i], dst_ref=parts.at[i],
            send_sem=parts_sem.at[0, i], recv_sem=parts_sem.at[1, i],
            device_id={"ctx": row_seat(i), "head": me}, device_id_type=MESH,
        ).wait_recv()

    def send_sum(i):
        return pltpu.make_async_remote_copy(
            src_ref=sums.at[i], dst_ref=low.at[0, part(seat), :],
            send_sem=sums_sem.at[0, i], recv_sem=sums_sem.at[1, seat],
            device_id={"ctx": row_seat(i), "head": me}, device_id_type=MESH,
        )

    def sum_arrived(i):
        i = lax.rem(seat + i, SEATS)
        piece = low.at[0, part(i), :]
        pltpu.make_async_remote_copy(
            src_ref=piece, dst_ref=piece,
            send_sem=sums_sem.at[0, i], recv_sem=sums_sem.at[1, i],
            device_id={"ctx": row_seat(i), "head": me}, device_id_type=MESH,
        ).wait_recv()

    def to_others(start, first, last):
        def step(i, _):
            @pl.when(i != seat)
            def _():
                start(i)

            return 0

        lax.fori_loop(first, last, step, 0)

    for load in loads[:3]:
        load.wait()
    lax.fori_loop(0, 2, key_side, 0)
    pl.semaphore_wait(barrier, 16)
    to_others(lambda i: send_part(i).start(), 0, 4)
    lax.fori_loop(2, 4, key_side, 0)
    to_others(lambda i: send_part(i).start(), 4, 8)
    for i in (1, 2, 3):
        w_z(i).start()
    parts[seat] = total[part(seat), :]

    loads[3].wait()
    loads[4].wait()

    def query_side(h, _):
        features(q_ref, qf, h)
        return 0

    lax.fori_loop(0, HEADS, query_side, 0)

    for i in range(1, SEATS):
        part_arrived(i)
    row_total = parts[0].astype(F32)
    for i in range(1, SEATS):
        row_total = row_total + parts[i].astype(F32)
    row_out[...] = row_total.astype(BF16)

    def send_row(i):
        return remote(row_out, row_in.at[i - 1], row_sem, i - 1, along_y(i))

    for i in (2, 1, 3):
        send_row(i).start()

    causal = (
        lax.broadcasted_iota(jnp.int32, (TILE, TILE), 0)
        >= lax.broadcasted_iota(jnp.int32, (TILE, TILE), 1)
    )

    def attend(n, _):
        h, b = n // 2, lax.rem(n, 2)
        upper, lower = tile_rows(2 * b), tile_rows(2 * b + 1)

        def scores(rows, cols, masked):
            s = dot(qf[h, rows, :], kf[h, cols, :], ((1,), (1,)))
            return (jnp.where(causal, s, 0.0) if masked else s).astype(BF16)

        v0, v1 = v_ref[upper, columns(h)], v_ref[lower, columns(h)]
        local[upper, columns(h)] = dot(scores(upper, upper, True), v0)
        local[lower, columns(h)] = dot(scores(lower, upper, False), v0) + dot(
            scores(lower, lower, True), v1
        )
        return 0

    lax.fori_loop(0, 3, attend, 0)

    for i in (1, 2, 3):
        send_row(i).wait()
    running = jnp.zeros((PART, FEATS), F32)
    for i in (1, 2, 3):
        running = running + jnp.where(y >= i, row_in[i - 1].astype(F32), 0.0)
    for i in range(SEATS):
        sums[i] = running.astype(BF16)
        if i < SEATS - 1:
            running = running + parts[i].astype(F32)
    to_others(lambda i: send_sum(i).start(), 0, 8)
    low[0, part(seat), :] = sums[seat]
    for i in (1, 2, 3):
        w_z_arrived(i)
        for o in (2, 1, 3):
            w_first(i, o).start()
    lax.fori_loop(3, 8, attend, 0)
    for i in range(1, SEATS):
        sum_arrived(i)
    low[1] = (low[0].astype(F32) + state[0]).astype(BF16)

    def half(q, t):
        return pl.ds(pl.multiple_of(q * TILE + t * HALF, HALF), HALF)

    def stored(slot, t):
        return full.at[lax.rem(slot + RING, RING), t * HALF : (t + 1) * HALF, :]

    def to_pair(t, k):
        target = mate if k == 0 else lax.rem(me + sign * {1: -1, 2: 2, 3: -3}[k] + RING, RING)
        piece = normed.at[half(target // 2, t), :]
        return remote_z(piece, stored(me, t), rows_sem.at[t], k, target)

    def rows_arrived(t, k):
        piece = stored(mate if k == 0 else me - sign * k, t)
        remote_z(piece, piece, rows_sem.at[t], k, mate).wait_recv()

    def pass_on(t, k):
        piece = stored(me - sign * k, t)
        return remote_z(piece, piece, pass_sem.at[t], k - 1, mate)

    def forward(t, k):
        rows_arrived(t, k)
        pass_on(t, k).start()

    def passed(t):
        for k in (1, 2, 3):
            piece = stored(me + sign * (k + 1), t)
            remote_z(piece, piece, pass_sem.at[t], k - 1, mate).wait_recv()

    def finish(q):
        rows = tile_rows(q)
        for h in range(HEADS):
            cols = slice(h * HDIM, (h + 1) * HDIM)
            attended = local[rows, cols] + dot(
                qf[h, rows, :], low[q // 2, h * HDIM : (h + 1) * HDIM, :], ((1,), (1,))
            )
            square = jnp.mean(attended * attended, axis=-1, keepdims=True)
            gain = gain_ref[cols].astype(F32).reshape(1, HDIM)
            normed[rows, cols] = (attended * lax.rsqrt(square + 1e-06) * gain).astype(BF16)

    def line(i):
        for o in (1, 2, 3):
            w_first_arrived(i, o)
        for o in (1, 3):
            w_second(i, o).start()
        w_core(i, 0).start()

    def relay(i):
        for d, o in ((0, 1), (1, 3)):
            w_second_arrived(i, o)
            w_relay(i, d).start()
            w_core(i, o).start()

    def halves(i):
        for d in (0, 1):
            w_relay_arrived(i, d)
        w_core(i, 2).start()

    def project(slot, target, t):
        rows = slice(t * HALF, (t + 1) * HALF)
        for s in (0, 2, 4, 6):
            term = dot(full[s, rows, :], w_ref[slot, s * 512 : s * 512 + 512, :]) + dot(
                full[s + 1, rows, :], w_ref[slot, s * 512 + 512 : s * 512 + 1024, :]
            )
            if s == 0:
                acc[...] = term
            elif s < 6:
                acc[...] += term
            else:
                out_ref[target, rows, :] = (acc[...] + term).astype(BF16)

    def back(t, i):
        return remote_z(
            out_ref.at[i, t * HALF : (t + 1) * HALF, :], out_hbm.at[half(pair, t), :],
            back_sem.at[t], i - 1, member(slot_of(i)),
        )

    def back_arrived(t, i):
        r = lax.rem(pair + i, 4)
        piece = out_hbm.at[half(r, t), :]
        remote_z(
            out_ref.at[i, t * HALF : (t + 1) * HALF, :], piece, back_sem.at[t], i - 1, member(r)
        ).wait_recv()

    def give_back(t, i):
        project(slot_of(i), i, t)
        back(t, i).start()

    line(1)
    for k, step in ((3, 2), (2, sign), (1, -sign), (0, 0)):
        finish(lax.rem(pair + step + 4, 4))
        to_pair(0, k).start()
    to_pair(1, 0).start()
    full[me] = normed[tile_rows(pair), :]

    line(2)
    line(3)
    forward(0, 1)
    forward(0, 2)
    forward(0, 3)
    for k in (3, 2, 1):
        to_pair(1, k).start()
    for i in (1, 2, 3):
        relay(i)
    rows_arrived(0, 0)
    halves(1)
    passed(0)
    w_core_arrived(1)
    give_back(0, 1)
    forward(1, 1)
    halves(2)
    w_core_arrived(2)
    give_back(0, 2)
    forward(1, 2)
    loads[5].wait()
    project(pair, 0, 0)
    forward(1, 3)
    halves(3)
    rows_arrived(1, 0)
    w_core_arrived(3)
    give_back(0, 3)
    passed(1)
    for i in (1, 2, 3):
        give_back(1, i)
    project(pair, 0, 1)
    keep = pltpu.make_async_copy(out_ref.at[0], out_hbm.at[tile_rows(pair), :], load_sem.at[0])
    keep.start()

    for i in (1, 2, 3):
        w_z(i).wait_send()
        for o in (0, 1, 2, 3):
            w_core(i, o).wait_send()
        for o in (1, 2, 3):
            w_first(i, o).wait_send()
        for d, o in ((0, 1), (1, 3)):
            w_second(i, o).wait_send()
            w_relay(i, d).wait_send()
    for t in (0, 1):
        for k in (1, 2, 3):
            pass_on(t, k).wait_send()
        for k in (0, 1, 2, 3):
            to_pair(t, k).wait_send()
    to_others(lambda i: send_part(i).wait_send(), 0, 8)
    to_others(lambda i: send_sum(i).wait_send(), 0, 8)
    keep.wait()
    for t in (0, 1):
        for i in (1, 2, 3):
            back(t, i).wait_send()
            back_arrived(t, i)


def local(query_rows, key_rows, value_rows, frequencies, norm_gain, out_weight):
    anywhere = pl.BlockSpec(memory_space=pl.ANY)
    operands = [
        pltpu.with_memory_space_constraint(operand, pltpu.HBM)
        for operand in (query_rows, key_rows, value_rows, frequencies, norm_gain, out_weight)
    ]
    return pl.pallas_call(
        kernel,
        out_shape=jax.ShapeDtypeStruct((ROWS, 512), BF16),
        in_specs=[anywhere] * 6,
        out_specs=anywhere,
        scratch_shapes=[
            pltpu.VMEM((ROWS, 512), BF16),
            pltpu.VMEM((ROWS, 512), BF16),
            pltpu.VMEM((ROWS, 512), BF16),
            pltpu.VMEM((HEADS, HDIM, HDIM), BF16),
            pltpu.VMEM((512,), BF16),
            pltpu.VMEM((4, 4096, 512), BF16),
            pltpu.VMEM((HEADS, ROWS, FEATS), BF16),
            pltpu.VMEM((HEADS, ROWS, FEATS), BF16),
            pltpu.VMEM((2, 512, FEATS), F32),
            pltpu.VMEM((ROWS, 512), F32),
            pltpu.VMEM((ROWS, 512), BF16),
            pltpu.VMEM((RING, TILE, 512), BF16),
            pltpu.VMEM((HALF, 512), F32),
            pltpu.VMEM((4, TILE, 512), BF16),
            pltpu.VMEM((512, FEATS), BF16),
            pltpu.VMEM((SEATS, PART, FEATS), BF16),
            pltpu.VMEM((PART, FEATS), BF16),
            pltpu.VMEM((3, PART, FEATS), BF16),
            pltpu.VMEM((SEATS, PART, FEATS), BF16),
            pltpu.VMEM((2, 512, FEATS), BF16),
            pltpu.SemaphoreType.DMA((6,)),
            pltpu.SemaphoreType.DMA((2, SEATS)),
            pltpu.SemaphoreType.DMA((2, 3)),
            pltpu.SemaphoreType.DMA((2, SEATS)),
            pltpu.SemaphoreType.DMA((2, 3)),
            pltpu.SemaphoreType.DMA((3, 2, 3)),
            pltpu.SemaphoreType.DMA((3, 2, 3)),
            pltpu.SemaphoreType.DMA((3, 2, 2)),
            pltpu.SemaphoreType.DMA((3, 2, 4)),
            pltpu.SemaphoreType.DMA((2, 2, 4)),
            pltpu.SemaphoreType.DMA((2, 2, 3)),
            pltpu.SemaphoreType.DMA((2, 2, 3)),
        ],
        compiler_params=pltpu.CompilerParams(
            collective_id=0, has_side_effects=True, vmem_limit_bytes=50 * 2**20
        ),
        cost_estimate=pl.CostEstimate(
            flops=7 * 10**9, bytes_accessed=9 * 2**20, transcendentals=0
        ),
    )(*operands)


def solution(mesh):
    return jax.shard_map(
        local,
        mesh=mesh,
        in_specs=(
            P("ctx", "head"),
            P("ctx", "head"),
            P("ctx", "head"),
            P("head", None, None),
            P("head"),
            P(None, "head"),
        ),
        out_specs=P("ctx", "head"),
        check_vma=False,
    )
```

```python
import functools
import math

import jax
import jax.numpy as jnp
from jax import lax
from jax.experimental import pallas as pl
from jax.experimental.pallas import tpu as pltpu
from jax.sharding import PartitionSpec as P

MESH = pl.DeviceIdType.MESH
F32 = jnp.float32
BF16 = jnp.bfloat16
HEADS = 4
HDIM = 128
FEATS = 256
ROWS = 1024
BLOCK = 512
TILE = 256
PIECES = 4
RING = 8
SLICE = 128
SEATS = 8
PART = 64
HALF = 128

TWO_PI_HIGH = 6.28125
TWO_PI_LOW = 2.0 * math.pi - TWO_PI_HIGH
ROUNDER = 12582912.0
SCALE = 1.0 / math.sqrt(128.0)


def half_angle_tables():
    import numpy as np

    root = math.sqrt(2.0 * SCALE)
    nodes = np.cos(np.pi * (np.arange(400) + 0.5) / 400.0) * np.pi**2 * 0.5 + np.pi**2 * 0.5
    angle = np.sqrt(nodes)
    cheb = np.polynomial.chebyshev.Chebyshev
    sine = cheb.fit(nodes, root * np.sin(angle / 2.0) / angle, 4, domain=[0.0, np.pi**2])
    cosine = cheb.fit(nodes, root * np.cos(angle / 2.0), 4, domain=[0.0, np.pi**2])
    poly = np.polynomial.Polynomial
    return (
        [float(v) for v in sine.convert(kind=poly, domain=[-1, 1]).coef],
        [float(v) for v in cosine.convert(kind=poly, domain=[-1, 1]).coef],
    )


SINE, COSINE = half_angle_tables()


def horner(z, table):
    out = z * table[-1] + table[-2]
    for value in table[-3::-1]:
        out = out * z + value
    return out


def cos_sin(phase):
    turns = (phase * (1.0 / (2.0 * math.pi)) + ROUNDER) - ROUNDER
    r = (phase - turns * TWO_PI_HIGH) - turns * TWO_PI_LOW
    z = r * r
    s = r * horner(z, SINE)
    c = horner(z, COSINE)
    return SCALE - s * s, s * c


def dot(a, b, dims=((1,), (0,))):
    return lax.dot_general(a, b, (dims, ((), ())), preferred_element_type=F32)


def columns(h):
    return pl.ds(pl.multiple_of(h * HDIM, HDIM), HDIM)


def tile_rows(p):
    return pl.ds(pl.multiple_of(p * TILE, TILE), TILE)


def kernel(
    q_hbm, k_hbm, v_hbm, freq_hbm, gain_hbm, w_hbm, out_hbm,
    q_ref, k_ref, v_ref, freq_ref, gain_ref, w_ref, qf, kf, state, local, normed, full, acc, out_ref,
    total, parts, row_out, row_in, sums, low,
    load_sem, parts_sem, row_sem, sums_sem,
    w_z_sem, w_first_sem, w_second_sem, w_relay_sem, w_core_sem, rows_sem, pass_sem, back_sem,
):
    ctx = lax.axis_index("ctx")
    me = lax.axis_index("head")
    core = lax.rem(ctx, 2)
    x = lax.rem(ctx // 2, 4)
    y = ctx // 8
    pair = me // 2
    sign = 1 - 2 * lax.rem(me, 2)
    mate = lax.rem(me + sign + RING, RING)

    def member(r):
        return 2 * r + lax.rem(me + pair // 2 + r // 2, 2)

    def at(y_, x_, core_):
        return (y_ * 4 + x_) * 2 + core_

    def row_seat(i):
        return y * SEATS + lax.rem(i, SEATS)

    def along_y(i):
        return at(lax.rem(y + i, 4), x, core)

    other = at(y, x, 1 - core)
    seat = 2 * x + core

    loads = [
        pltpu.make_async_copy(src, dst, load_sem.at[i])
        for i, (src, dst) in enumerate(
            (
                (freq_hbm, freq_ref), (k_hbm, k_ref), (v_hbm, v_ref), (q_hbm, q_ref),
                (gain_hbm, gain_ref), (w_hbm, w_ref.at[pair]),
            )
        )
    ]
    for load in loads:
        load.start()

    barrier = pltpu.get_barrier_semaphore()

    def greet(c_, h_):
        pl.semaphore_signal(
            barrier, inc=1, device_id={"ctx": c_, "head": h_}, device_id_type=MESH
        )

    for i in range(1, SEATS):
        greet(row_seat(seat + i), me)
    for i in (1, 2, 3):
        greet(along_y(i), me)
    for i in (1, 2, 3, 5, 6, 7):
        greet(ctx, lax.rem(me + i, RING))

    def remote(src, dst, sems, slot, c_):
        return pltpu.make_async_remote_copy(
            src_ref=src, dst_ref=dst, send_sem=sems.at[0, slot], recv_sem=sems.at[1, slot],
            device_id={"ctx": c_, "head": me}, device_id_type=MESH,
        )

    def remote_z(src, dst, sems, slot, h_):
        return pltpu.make_async_remote_copy(
            src_ref=src, dst_ref=dst, send_sem=sems.at[0, slot], recv_sem=sems.at[1, slot],
            device_id={"ctx": ctx, "head": h_}, device_id_type=MESH,
        )

    def first_peer(i):
        return at(lax.rem(y + core * i, 4), lax.rem(x + (1 - core) * i, 4), core)

    def second_peer(i):
        return at(lax.rem(y + (1 - core) * i, 4), lax.rem(x + core * i, 4), core)

    first_place = core * y + (1 - core) * x
    second_place = core * x + (1 - core) * y
    half_rows = core * 2048

    def slot_of(i):
        return lax.rem(pair + 4 - i, 4)

    def w_piece(i, start, size):
        return w_ref.at[slot_of(i), pl.ds(pl.multiple_of(start, SLICE), size), :]

    line_start = half_rows + second_place * 512
    slice_start = line_start + first_place * SLICE

    def w_z(i):
        rows = pl.ds(pl.multiple_of(slice_start, SLICE), SLICE)
        return remote_z(
            w_hbm.at[rows, :], w_ref.at[pair, rows, :], w_z_sem, i - 1, member(lax.rem(pair + i, 4))
        )

    def w_z_arrived(i):
        piece = w_piece(i, slice_start, SLICE)
        remote_z(piece, piece, w_z_sem, i - 1, member(slot_of(i))).wait_recv()

    def w_first(i, o):
        piece = w_piece(i, slice_start, SLICE)
        return remote(piece, piece, w_first_sem.at[i - 1], o - 1, first_peer(o))

    def w_first_arrived(i, o):
        piece = w_piece(i, line_start + lax.rem(first_place + 4 - o, 4) * SLICE, SLICE)
        remote(piece, piece, w_first_sem.at[i - 1], o - 1, first_peer(o)).wait_recv()

    def w_second(i, o):
        piece = w_piece(i, line_start, 512)
        return remote(piece, piece, w_second_sem.at[i - 1], o - 1, second_peer(o))

    def w_second_arrived(i, o):
        piece = w_piece(i, half_rows + lax.rem(second_place + 4 - o, 4) * 512, 512)
        remote(piece, piece, w_second_sem.at[i - 1], o - 1, second_peer(o)).wait_recv()

    def w_relay(i, d):
        source = lax.rem(second_place + (3 if d == 0 else 1), 4)
        piece = w_piece(i, half_rows + source * 512 + d * 256, 256)
        return remote(piece, piece, w_relay_sem.at[i - 1], d, second_peer(1 if d == 0 else 3))

    def w_relay_arrived(i, d):
        piece = w_piece(i, half_rows + lax.rem(second_place + 2, 4) * 512 + d * 256, 256)
        remote(piece, piece, w_relay_sem.at[i - 1], d, second_peer(1)).wait_recv()

    def w_core(i, o):
        piece = w_piece(i, half_rows + lax.rem(second_place + 4 - o, 4) * 512, 512)
        return remote(piece, piece, w_core_sem.at[i - 1], o, other)

    def w_core_arrived(i):
        for o in (0, 1, 2, 3):
            piece = w_piece(i, 2048 - half_rows + o * 512, 512)
            remote(piece, piece, w_core_sem.at[i - 1], o, other).wait_recv()

    def features(rows_ref, feat_ref, h):
        def chunk(p, _):
            phase = dot(rows_ref[tile_rows(p), columns(h)], freq_ref[h])
            cosine, sine = cos_sin(phase)
            feat_ref[h, tile_rows(p), 0:128] = cosine.astype(BF16)
            feat_ref[h, tile_rows(p), 128:256] = sine.astype(BF16)
            return 0

        lax.fori_loop(0, PIECES, chunk, 0, unroll=True)

    def head_rows(h):
        return pl.ds(pl.multiple_of(h * HDIM, HDIM), HDIM)

    def part(i):
        return pl.ds(pl.multiple_of(i * PART, PART), PART)

    def key_side(h, _):
        features(k_ref, kf, h)
        for b in (0, 1):
            rows = slice(b * BLOCK, (b + 1) * BLOCK)
            state[b, head_rows(h), :] = dot(v_ref[rows, columns(h)], kf[h, rows, :], ((0,), (0,)))
        total[head_rows(h), :] = (state[0, head_rows(h), :] + state[1, head_rows(h), :]).astype(BF16)
        return 0

    def send_part(i):
        return pltpu.make_async_remote_copy(
            src_ref=total.at[part(i), :], dst_ref=parts.at[seat],
            send_sem=parts_sem.at[0, i], recv_sem=parts_sem.at[1, seat],
            device_id={"ctx": row_seat(i), "head": me}, device_id_type=MESH,
        )

    def part_arrived(i):
        i = lax.rem(seat + i, SEATS)
        pltpu.make_async_remote_copy(
            src_ref=parts.at[i], dst_ref=parts.at[i],
            send_sem=parts_sem.at[0, i], recv_sem=parts_sem.at[1, i],
            device_id={"ctx": row_seat(i), "head": me}, device_id_type=MESH,
        ).wait_recv()

    def send_sum(i):
        return pltpu.make_async_remote_copy(
            src_ref=sums.at[i], dst_ref=low.at[0, part(seat), :],
            send_sem=sums_sem.at[0, i], recv_sem=sums_sem.at[1, seat],
            device_id={"ctx": row_seat(i), "head": me}, device_id_type=MESH,
        )

    def sum_arrived(i):
        i = lax.rem(seat + i, SEATS)
        piece = low.at[0, part(i), :]
        pltpu.make_async_remote_copy(
            src_ref=piece, dst_ref=piece,
            send_sem=sums_sem.at[0, i], recv_sem=sums_sem.at[1, i],
            device_id={"ctx": row_seat(i), "head": me}, device_id_type=MESH,
        ).wait_recv()

    def to_others(start, first, last):
        def step(i, _):
            @pl.when(i != seat)
            def _():
                start(i)

            return 0

        lax.fori_loop(first, last, step, 0)

    for load in loads[:3]:
        load.wait()
    lax.fori_loop(0, 2, key_side, 0)
    pl.semaphore_wait(barrier, 16)
    to_others(lambda i: send_part(i).start(), 0, 4)
    lax.fori_loop(2, 4, key_side, 0)
    to_others(lambda i: send_part(i).start(), 4, 8)
    for i in (1, 2, 3):
        w_z(i).start()
    parts[seat] = total[part(seat), :]

    loads[3].wait()
    loads[4].wait()

    def query_side(h, _):
        features(q_ref, qf, h)
        return 0

    lax.fori_loop(0, HEADS, query_side, 0)

    for i in range(1, SEATS):
        part_arrived(i)
    row_total = parts[0].astype(F32)
    for i in range(1, SEATS):
        row_total = row_total + parts[i].astype(F32)
    row_out[...] = row_total.astype(BF16)

    def send_row(i):
        return remote(row_out, row_in.at[i - 1], row_sem, i - 1, along_y(i))

    for i in (2, 1, 3):
        send_row(i).start()

    causal = (
        lax.broadcasted_iota(jnp.int32, (TILE, TILE), 0)
        >= lax.broadcasted_iota(jnp.int32, (TILE, TILE), 1)
    )

    def attend(n, _):
        h, b = n // 2, lax.rem(n, 2)
        upper, lower = tile_rows(2 * b), tile_rows(2 * b + 1)

        def scores(rows, cols, masked):
            s = dot(qf[h, rows, :], kf[h, cols, :], ((1,), (1,)))
            return (jnp.where(causal, s, 0.0) if masked else s).astype(BF16)

        v0, v1 = v_ref[upper, columns(h)], v_ref[lower, columns(h)]
        local[upper, columns(h)] = dot(scores(upper, upper, True), v0)
        local[lower, columns(h)] = dot(scores(lower, upper, False), v0) + dot(
            scores(lower, lower, True), v1
        )
        return 0

    lax.fori_loop(0, 3, attend, 0)

    for i in (1, 2, 3):
        send_row(i).wait()
    running = jnp.zeros((PART, FEATS), F32)
    for i in (1, 2, 3):
        running = running + jnp.where(y >= i, row_in[i - 1].astype(F32), 0.0)
    for i in range(SEATS):
        sums[i] = running.astype(BF16)
        if i < SEATS - 1:
            running = running + parts[i].astype(F32)
    to_others(lambda i: send_sum(i).start(), 0, 8)
    low[0, part(seat), :] = sums[seat]
    for i in (1, 2, 3):
        w_z_arrived(i)
        for o in (2, 1, 3):
            w_first(i, o).start()
    lax.fori_loop(3, 8, attend, 0)
    for i in range(1, SEATS):
        sum_arrived(i)
    low[1] = (low[0].astype(F32) + state[0]).astype(BF16)

    def half(q, t):
        return pl.ds(pl.multiple_of(q * TILE + t * HALF, HALF), HALF)

    def stored(slot, t):
        return full.at[lax.rem(slot + RING, RING), t * HALF : (t + 1) * HALF, :]

    def to_pair(t, k):
        target = mate if k == 0 else lax.rem(me + sign * {1: -1, 2: 2, 3: -3}[k] + RING, RING)
        piece = normed.at[half(target // 2, t), :]
        return remote_z(piece, stored(me, t), rows_sem.at[t], k, target)

    def rows_arrived(t, k):
        piece = stored(mate if k == 0 else me - sign * k, t)
        remote_z(piece, piece, rows_sem.at[t], k, mate).wait_recv()

    def pass_on(t, k):
        piece = stored(me - sign * k, t)
        return remote_z(piece, piece, pass_sem.at[t], k - 1, mate)

    def forward(t, k):
        rows_arrived(t, k)
        pass_on(t, k).start()

    def passed(t):
        for k in (1, 2, 3):
            piece = stored(me + sign * (k + 1), t)
            remote_z(piece, piece, pass_sem.at[t], k - 1, mate).wait_recv()

    def finish(q):
        rows = tile_rows(q)
        for h in range(HEADS):
            cols = slice(h * HDIM, (h + 1) * HDIM)
            attended = local[rows, cols] + dot(
                qf[h, rows, :], low[q // 2, h * HDIM : (h + 1) * HDIM, :], ((1,), (1,))
            )
            square = jnp.mean(attended * attended, axis=-1, keepdims=True)
            gain = gain_ref[cols].astype(F32).reshape(1, HDIM)
            normed[rows, cols] = (attended * lax.rsqrt(square + 1e-06) * gain).astype(BF16)

    def line(i):
        for o in (1, 2, 3):
            w_first_arrived(i, o)
        for o in (1, 3):
            w_second(i, o).start()
        w_core(i, 0).start()

    def relay(i):
        for d, o in ((0, 1), (1, 3)):
            w_second_arrived(i, o)
            w_relay(i, d).start()
            w_core(i, o).start()

    def halves(i):
        for d in (0, 1):
            w_relay_arrived(i, d)
        w_core(i, 2).start()

    def project(slot, target, t):
        rows = slice(t * HALF, (t + 1) * HALF)
        for s in (0, 2, 4, 6):
            term = dot(full[s, rows, :], w_ref[slot, s * 512 : s * 512 + 512, :]) + dot(
                full[s + 1, rows, :], w_ref[slot, s * 512 + 512 : s * 512 + 1024, :]
            )
            if s == 0:
                acc[...] = term
            elif s < 6:
                acc[...] += term
            else:
                out_ref[target, rows, :] = (acc[...] + term).astype(BF16)

    def back(t, i):
        return remote_z(
            out_ref.at[i, t * HALF : (t + 1) * HALF, :], out_hbm.at[half(pair, t), :],
            back_sem.at[t], i - 1, member(slot_of(i)),
        )

    def back_arrived(t, i):
        r = lax.rem(pair + i, 4)
        piece = out_hbm.at[half(r, t), :]
        remote_z(
            out_ref.at[i, t * HALF : (t + 1) * HALF, :], piece, back_sem.at[t], i - 1, member(r)
        ).wait_recv()

    def give_back(t, i):
        project(slot_of(i), i, t)
        back(t, i).start()

    line(1)
    for k, step in ((3, 2), (2, sign), (1, -sign), (0, 0)):
        finish(lax.rem(pair + step + 4, 4))
        to_pair(0, k).start()
    to_pair(1, 0).start()
    full[me] = normed[tile_rows(pair), :]

    line(2)
    line(3)
    forward(0, 1)
    forward(0, 2)
    forward(0, 3)
    relay(1)
    for k in (3, 2, 1):
        to_pair(1, k).start()
    relay(2)
    relay(3)
    rows_arrived(0, 0)
    halves(1)
    passed(0)
    forward(1, 1)
    forward(1, 2)
    w_core_arrived(1)
    give_back(0, 1)
    halves(2)
    forward(1, 3)
    w_core_arrived(2)
    give_back(0, 2)
    loads[5].wait()
    project(pair, 0, 0)
    halves(3)
    rows_arrived(1, 0)
    w_core_arrived(3)
    give_back(0, 3)
    passed(1)
    for i in (1, 2, 3):
        give_back(1, i)
    project(pair, 0, 1)
    keep = pltpu.make_async_copy(out_ref.at[0], out_hbm.at[tile_rows(pair), :], load_sem.at[0])
    keep.start()

    for i in (1, 2, 3):
        w_z(i).wait_send()
        for o in (0, 1, 2, 3):
            w_core(i, o).wait_send()
        for o in (1, 2, 3):
            w_first(i, o).wait_send()
        for d, o in ((0, 1), (1, 3)):
            w_second(i, o).wait_send()
            w_relay(i, d).wait_send()
    for t in (0, 1):
        for k in (1, 2, 3):
            pass_on(t, k).wait_send()
        for k in (0, 1, 2, 3):
            to_pair(t, k).wait_send()
    to_others(lambda i: send_part(i).wait_send(), 0, 8)
    to_others(lambda i: send_sum(i).wait_send(), 0, 8)
    keep.wait()
    for t in (0, 1):
        for i in (1, 2, 3):
            back(t, i).wait_send()
            back_arrived(t, i)


def local(query_rows, key_rows, value_rows, frequencies, norm_gain, out_weight):
    anywhere = pl.BlockSpec(memory_space=pl.ANY)
    operands = [
        pltpu.with_memory_space_constraint(operand, pltpu.HBM)
        for operand in (query_rows, key_rows, value_rows, frequencies, norm_gain, out_weight)
    ]
    return pl.pallas_call(
        kernel,
        out_shape=jax.ShapeDtypeStruct((ROWS, 512), BF16),
        in_specs=[anywhere] * 6,
        out_specs=anywhere,
        scratch_shapes=[
            pltpu.VMEM((ROWS, 512), BF16),
            pltpu.VMEM((ROWS, 512), BF16),
            pltpu.VMEM((ROWS, 512), BF16),
            pltpu.VMEM((HEADS, HDIM, HDIM), BF16),
            pltpu.VMEM((512,), BF16),
            pltpu.VMEM((4, 4096, 512), BF16),
            pltpu.VMEM((HEADS, ROWS, FEATS), BF16),
            pltpu.VMEM((HEADS, ROWS, FEATS), BF16),
            pltpu.VMEM((2, 512, FEATS), F32),
            pltpu.VMEM((ROWS, 512), F32),
            pltpu.VMEM((ROWS, 512), BF16),
            pltpu.VMEM((RING, TILE, 512), BF16),
            pltpu.VMEM((HALF, 512), F32),
            pltpu.VMEM((4, TILE, 512), BF16),
            pltpu.VMEM((512, FEATS), BF16),
            pltpu.VMEM((SEATS, PART, FEATS), BF16),
            pltpu.VMEM((PART, FEATS), BF16),
            pltpu.VMEM((3, PART, FEATS), BF16),
            pltpu.VMEM((SEATS, PART, FEATS), BF16),
            pltpu.VMEM((2, 512, FEATS), BF16),
            pltpu.SemaphoreType.DMA((6,)),
            pltpu.SemaphoreType.DMA((2, SEATS)),
            pltpu.SemaphoreType.DMA((2, 3)),
            pltpu.SemaphoreType.DMA((2, SEATS)),
            pltpu.SemaphoreType.DMA((2, 3)),
            pltpu.SemaphoreType.DMA((3, 2, 3)),
            pltpu.SemaphoreType.DMA((3, 2, 3)),
            pltpu.SemaphoreType.DMA((3, 2, 2)),
            pltpu.SemaphoreType.DMA((3, 2, 4)),
            pltpu.SemaphoreType.DMA((2, 2, 4)),
            pltpu.SemaphoreType.DMA((2, 2, 3)),
            pltpu.SemaphoreType.DMA((2, 2, 3)),
        ],
        compiler_params=pltpu.CompilerParams(
            collective_id=0, has_side_effects=True, vmem_limit_bytes=50 * 2**20
        ),
        cost_estimate=pl.CostEstimate(
            flops=7 * 10**9, bytes_accessed=9 * 2**20, transcendentals=0
        ),
    )(*operands)


def solution(mesh):
    return jax.shard_map(
        local,
        mesh=mesh,
        in_specs=(
            P("ctx", "head"),
            P("ctx", "head"),
            P("ctx", "head"),
            P("head", None, None),
            P("head"),
            P(None, "head"),
        ),
        out_specs=P("ctx", "head"),
        check_vma=False,
    )
```

```python
import functools
import math

import jax
import jax.numpy as jnp
from jax import lax
from jax.experimental import pallas as pl
from jax.experimental.pallas import tpu as pltpu
from jax.sharding import PartitionSpec as P

MESH = pl.DeviceIdType.MESH
F32 = jnp.float32
BF16 = jnp.bfloat16
HEADS = 4
HDIM = 128
FEATS = 256
ROWS = 1024
BLOCK = 512
TILE = 256
PIECES = 4
RING = 8
SLICE = 128
SEATS = 8
PART = 64
HALF = 128

TWO_PI_HIGH = 6.28125
TWO_PI_LOW = 2.0 * math.pi - TWO_PI_HIGH
ROUNDER = 12582912.0
SCALE = 1.0 / math.sqrt(128.0)


def half_angle_tables():
    import numpy as np

    root = math.sqrt(2.0 * SCALE)
    nodes = np.cos(np.pi * (np.arange(400) + 0.5) / 400.0) * np.pi**2 * 0.5 + np.pi**2 * 0.5
    angle = np.sqrt(nodes)
    cheb = np.polynomial.chebyshev.Chebyshev
    sine = cheb.fit(nodes, root * np.sin(angle / 2.0) / angle, 4, domain=[0.0, np.pi**2])
    cosine = cheb.fit(nodes, root * np.cos(angle / 2.0), 4, domain=[0.0, np.pi**2])
    poly = np.polynomial.Polynomial
    return (
        [float(v) for v in sine.convert(kind=poly, domain=[-1, 1]).coef],
        [float(v) for v in cosine.convert(kind=poly, domain=[-1, 1]).coef],
    )


SINE, COSINE = half_angle_tables()


def horner(z, table):
    out = z * table[-1] + table[-2]
    for value in table[-3::-1]:
        out = out * z + value
    return out


def cos_sin(phase):
    turns = (phase * (1.0 / (2.0 * math.pi)) + ROUNDER) - ROUNDER
    r = (phase - turns * TWO_PI_HIGH) - turns * TWO_PI_LOW
    z = r * r
    s = r * horner(z, SINE)
    c = horner(z, COSINE)
    return SCALE - s * s, s * c


def dot(a, b, dims=((1,), (0,))):
    return lax.dot_general(a, b, (dims, ((), ())), preferred_element_type=F32)


def columns(h):
    return pl.ds(pl.multiple_of(h * HDIM, HDIM), HDIM)


def tile_rows(p):
    return pl.ds(pl.multiple_of(p * TILE, TILE), TILE)


def kernel(
    q_hbm, k_hbm, v_hbm, freq_hbm, gain_hbm, w_hbm, out_hbm,
    q_ref, k_ref, v_ref, freq_ref, gain_ref, w_ref, qf, kf, state, local, normed, full, acc, out_ref,
    total, parts, row_out, row_in, sums, low,
    load_sem, parts_sem, row_sem, sums_sem,
    w_z_sem, w_first_sem, w_second_sem, w_relay_sem, w_core_sem, rows_sem, pass_sem, back_sem,
):
    ctx = lax.axis_index("ctx")
    me = lax.axis_index("head")
    core = lax.rem(ctx, 2)
    x = lax.rem(ctx // 2, 4)
    y = ctx // 8
    pair = me // 2
    sign = 1 - 2 * lax.rem(me, 2)
    mate = lax.rem(me + sign + RING, RING)

    def member(r):
        return 2 * r + lax.rem(me + pair // 2 + r // 2, 2)

    def at(y_, x_, core_):
        return (y_ * 4 + x_) * 2 + core_

    def row_seat(i):
        return y * SEATS + lax.rem(i, SEATS)

    def along_y(i):
        return at(lax.rem(y + i, 4), x, core)

    other = at(y, x, 1 - core)
    seat = 2 * x + core

    loads = [
        pltpu.make_async_copy(src, dst, load_sem.at[i])
        for i, (src, dst) in enumerate(
            (
                (freq_hbm, freq_ref), (k_hbm, k_ref), (v_hbm, v_ref), (q_hbm, q_ref),
                (gain_hbm, gain_ref), (w_hbm, w_ref.at[pair]),
            )
        )
    ]
    for load in loads:
        load.start()

    barrier = pltpu.get_barrier_semaphore()

    def greet(c_, h_):
        pl.semaphore_signal(
            barrier, inc=1, device_id={"ctx": c_, "head": h_}, device_id_type=MESH
        )

    for i in range(1, SEATS):
        greet(row_seat(seat + i), me)
    for i in (1, 2, 3):
        greet(along_y(i), me)
    for i in (1, 2, 3, 5, 6, 7):
        greet(ctx, lax.rem(me + i, RING))

    def remote(src, dst, sems, slot, c_):
        return pltpu.make_async_remote_copy(
            src_ref=src, dst_ref=dst, send_sem=sems.at[0, slot], recv_sem=sems.at[1, slot],
            device_id={"ctx": c_, "head": me}, device_id_type=MESH,
        )

    def remote_z(src, dst, sems, slot, h_):
        return pltpu.make_async_remote_copy(
            src_ref=src, dst_ref=dst, send_sem=sems.at[0, slot], recv_sem=sems.at[1, slot],
            device_id={"ctx": ctx, "head": h_}, device_id_type=MESH,
        )

    def first_peer(i):
        return at(lax.rem(y + core * i, 4), lax.rem(x + (1 - core) * i, 4), core)

    def second_peer(i):
        return at(lax.rem(y + (1 - core) * i, 4), lax.rem(x + core * i, 4), core)

    first_place = core * y + (1 - core) * x
    second_place = core * x + (1 - core) * y
    half_rows = core * 2048

    def slot_of(i):
        return lax.rem(pair + 4 - i, 4)

    def w_piece(i, start, size):
        return w_ref.at[slot_of(i), pl.ds(pl.multiple_of(start, SLICE), size), :]

    line_start = half_rows + second_place * 512
    slice_start = line_start + first_place * SLICE

    def w_z(i):
        rows = pl.ds(pl.multiple_of(slice_start, SLICE), SLICE)
        return remote_z(
            w_hbm.at[rows, :], w_ref.at[pair, rows, :], w_z_sem, i - 1, member(lax.rem(pair + i, 4))
        )

    def w_z_arrived(i):
        piece = w_piece(i, slice_start, SLICE)
        remote_z(piece, piece, w_z_sem, i - 1, member(slot_of(i))).wait_recv()

    def w_first(i, o):
        piece = w_piece(i, slice_start, SLICE)
        return remote(piece, piece, w_first_sem.at[i - 1], o - 1, first_peer(o))

    def w_first_arrived(i, o):
        piece = w_piece(i, line_start + lax.rem(first_place + 4 - o, 4) * SLICE, SLICE)
        remote(piece, piece, w_first_sem.at[i - 1], o - 1, first_peer(o)).wait_recv()

    def w_second(i, o):
        piece = w_piece(i, line_start, 512)
        return remote(piece, piece, w_second_sem.at[i - 1], o - 1, second_peer(o))

    def w_second_arrived(i, o):
        piece = w_piece(i, half_rows + lax.rem(second_place + 4 - o, 4) * 512, 512)
        remote(piece, piece, w_second_sem.at[i - 1], o - 1, second_peer(o)).wait_recv()

    def w_relay(i, d):
        source = lax.rem(second_place + (3 if d == 0 else 1), 4)
        piece = w_piece(i, half_rows + source * 512 + d * 256, 256)
        return remote(piece, piece, w_relay_sem.at[i - 1], d, second_peer(1 if d == 0 else 3))

    def w_relay_arrived(i, d):
        piece = w_piece(i, half_rows + lax.rem(second_place + 2, 4) * 512 + d * 256, 256)
        remote(piece, piece, w_relay_sem.at[i - 1], d, second_peer(1)).wait_recv()

    def w_core(i, o):
        piece = w_piece(i, half_rows + lax.rem(second_place + 4 - o, 4) * 512, 512)
        return remote(piece, piece, w_core_sem.at[i - 1], o, other)

    def w_core_arrived(i):
        for o in (0, 1, 2, 3):
            piece = w_piece(i, 2048 - half_rows + o * 512, 512)
            remote(piece, piece, w_core_sem.at[i - 1], o, other).wait_recv()

    def features(rows_ref, feat_ref, h):
        def chunk(p, _):
            phase = dot(rows_ref[tile_rows(p), columns(h)], freq_ref[h])
            cosine, sine = cos_sin(phase)
            feat_ref[h, tile_rows(p), 0:128] = cosine.astype(BF16)
            feat_ref[h, tile_rows(p), 128:256] = sine.astype(BF16)
            return 0

        lax.fori_loop(0, PIECES, chunk, 0, unroll=True)

    def head_rows(h):
        return pl.ds(pl.multiple_of(h * HDIM, HDIM), HDIM)

    def part(i):
        return pl.ds(pl.multiple_of(i * PART, PART), PART)

    def key_side(h, _):
        features(k_ref, kf, h)
        for b in (0, 1):
            rows = slice(b * BLOCK, (b + 1) * BLOCK)
            state[b, head_rows(h), :] = dot(v_ref[rows, columns(h)], kf[h, rows, :], ((0,), (0,)))
        total[head_rows(h), :] = (state[0, head_rows(h), :] + state[1, head_rows(h), :]).astype(BF16)
        return 0

    def send_part(i):
        return pltpu.make_async_remote_copy(
            src_ref=total.at[part(i), :], dst_ref=parts.at[seat],
            send_sem=parts_sem.at[0, i], recv_sem=parts_sem.at[1, seat],
            device_id={"ctx": row_seat(i), "head": me}, device_id_type=MESH,
        )

    def part_arrived(i):
        i = lax.rem(seat + i, SEATS)
        pltpu.make_async_remote_copy(
            src_ref=parts.at[i], dst_ref=parts.at[i],
            send_sem=parts_sem.at[0, i], recv_sem=parts_sem.at[1, i],
            device_id={"ctx": row_seat(i), "head": me}, device_id_type=MESH,
        ).wait_recv()

    def send_sum(i):
        return pltpu.make_async_remote_copy(
            src_ref=sums.at[i], dst_ref=low.at[0, part(seat), :],
            send_sem=sums_sem.at[0, i], recv_sem=sums_sem.at[1, seat],
            device_id={"ctx": row_seat(i), "head": me}, device_id_type=MESH,
        )

    def sum_arrived(i):
        i = lax.rem(seat + i, SEATS)
        piece = low.at[0, part(i), :]
        pltpu.make_async_remote_copy(
            src_ref=piece, dst_ref=piece,
            send_sem=sums_sem.at[0, i], recv_sem=sums_sem.at[1, i],
            device_id={"ctx": row_seat(i), "head": me}, device_id_type=MESH,
        ).wait_recv()

    def to_others(start, first, last):
        def step(i, _):
            @pl.when(i != seat)
            def _():
                start(i)

            return 0

        lax.fori_loop(first, last, step, 0)

    for load in loads[:3]:
        load.wait()
    lax.fori_loop(0, 2, key_side, 0)
    pl.semaphore_wait(barrier, 16)
    to_others(lambda i: send_part(i).start(), 0, 4)
    lax.fori_loop(2, 4, key_side, 0)
    to_others(lambda i: send_part(i).start(), 4, 8)
    for i in (1, 2, 3):
        w_z(i).start()
    parts[seat] = total[part(seat), :]

    loads[3].wait()
    loads[4].wait()

    def query_side(h, _):
        features(q_ref, qf, h)
        return 0

    lax.fori_loop(0, HEADS, query_side, 0)

    for i in range(1, SEATS):
        part_arrived(i)
    row_total = parts[0].astype(F32)
    for i in range(1, SEATS):
        row_total = row_total + parts[i].astype(F32)
    row_out[...] = row_total.astype(BF16)

    def send_row(i):
        return remote(row_out, row_in.at[i - 1], row_sem, i - 1, along_y(i))

    for i in (2, 1, 3):
        send_row(i).start()

    causal = (
        lax.broadcasted_iota(jnp.int32, (TILE, TILE), 0)
        >= lax.broadcasted_iota(jnp.int32, (TILE, TILE), 1)
    )

    def attend(n, _):
        h, b = n // 2, lax.rem(n, 2)
        upper, lower = tile_rows(2 * b), tile_rows(2 * b + 1)

        def scores(rows, cols, masked):
            s = dot(qf[h, rows, :], kf[h, cols, :], ((1,), (1,)))
            return (jnp.where(causal, s, 0.0) if masked else s).astype(BF16)

        v0, v1 = v_ref[upper, columns(h)], v_ref[lower, columns(h)]
        local[upper, columns(h)] = dot(scores(upper, upper, True), v0)
        local[lower, columns(h)] = dot(scores(lower, upper, False), v0) + dot(
            scores(lower, lower, True), v1
        )
        return 0

    lax.fori_loop(0, 3, attend, 0)

    for i in (1, 2, 3):
        send_row(i).wait()
    running = jnp.zeros((PART, FEATS), F32)
    for i in (1, 2, 3):
        running = running + jnp.where(y >= i, row_in[i - 1].astype(F32), 0.0)
    for i in range(SEATS):
        sums[i] = running.astype(BF16)
        if i < SEATS - 1:
            running = running + parts[i].astype(F32)
    to_others(lambda i: send_sum(i).start(), 0, 8)
    low[0, part(seat), :] = sums[seat]
    for i in (1, 2, 3):
        w_z_arrived(i)
        for o in (2, 1, 3):
            w_first(i, o).start()
    lax.fori_loop(3, 8, attend, 0)
    for i in range(1, SEATS):
        sum_arrived(i)
    low[1] = (low[0].astype(F32) + state[0]).astype(BF16)

    def half(q, t):
        return pl.ds(pl.multiple_of(q * TILE + t * HALF, HALF), HALF)

    def stored(slot, t):
        return full.at[lax.rem(slot + RING, RING), t * HALF : (t + 1) * HALF, :]

    def to_pair(t, k):
        target = mate if k == 0 else lax.rem(me + sign * {1: -1, 2: 2, 3: -3}[k] + RING, RING)
        piece = normed.at[half(target // 2, t), :]
        return remote_z(piece, stored(me, t), rows_sem.at[t], k, target)

    def rows_arrived(t, k):
        piece = stored(mate if k == 0 else me - sign * k, t)
        remote_z(piece, piece, rows_sem.at[t], k, mate).wait_recv()

    def pass_on(t, k):
        piece = stored(me - sign * k, t)
        return remote_z(piece, piece, pass_sem.at[t], k - 1, mate)

    def forward(t, k):
        rows_arrived(t, k)
        pass_on(t, k).start()

    def passed(t):
        for k in (1, 2, 3):
            piece = stored(me + sign * (k + 1), t)
            remote_z(piece, piece, pass_sem.at[t], k - 1, mate).wait_recv()

    def finish(q):
        rows = tile_rows(q)
        for h in range(HEADS):
            cols = slice(h * HDIM, (h + 1) * HDIM)
            attended = local[rows, cols] + dot(
                qf[h, rows, :], low[q // 2, h * HDIM : (h + 1) * HDIM, :], ((1,), (1,))
            )
            square = jnp.mean(attended * attended, axis=-1, keepdims=True)
            gain = gain_ref[cols].astype(F32).reshape(1, HDIM)
            normed[rows, cols] = (attended * lax.rsqrt(square + 1e-06) * gain).astype(BF16)

    def line(i):
        for o in (1, 2, 3):
            w_first_arrived(i, o)
        for o in (1, 3):
            w_second(i, o).start()
        w_core(i, 0).start()

    def relay(i):
        for d, o in ((0, 1), (1, 3)):
            w_second_arrived(i, o)
            w_relay(i, d).start()
            w_core(i, o).start()

    def halves(i):
        for d in (0, 1):
            w_relay_arrived(i, d)
        w_core(i, 2).start()

    def project(slot, target, t):
        rows = slice(t * HALF, (t + 1) * HALF)
        for s in (0, 2, 4, 6):
            term = dot(full[s, rows, :], w_ref[slot, s * 512 : s * 512 + 512, :]) + dot(
                full[s + 1, rows, :], w_ref[slot, s * 512 + 512 : s * 512 + 1024, :]
            )
            if s == 0:
                acc[...] = term
            elif s < 6:
                acc[...] += term
            else:
                out_ref[target, rows, :] = (acc[...] + term).astype(BF16)

    def back(t, i):
        return remote_z(
            out_ref.at[i, t * HALF : (t + 1) * HALF, :], out_hbm.at[half(pair, t), :],
            back_sem.at[t], i - 1, member(slot_of(i)),
        )

    def back_arrived(t, i):
        r = lax.rem(pair + i, 4)
        piece = out_hbm.at[half(r, t), :]
        remote_z(
            out_ref.at[i, t * HALF : (t + 1) * HALF, :], piece, back_sem.at[t], i - 1, member(r)
        ).wait_recv()

    def give_back(t, i):
        project(slot_of(i), i, t)
        back(t, i).start()

    line(1)
    for k, step in ((3, 2), (2, sign), (1, -sign), (0, 0)):
        finish(lax.rem(pair + step + 4, 4))
        to_pair(0, k).start()
    full[me] = normed[tile_rows(pair), :]

    line(2)
    line(3)
    forward(0, 1)
    forward(0, 2)
    forward(0, 3)
    relay(1)
    for k in (3, 2, 1, 0):
        to_pair(1, k).start()
    relay(2)
    relay(3)
    rows_arrived(0, 0)
    halves(1)
    passed(0)
    forward(1, 1)
    forward(1, 2)
    w_core_arrived(1)
    give_back(0, 1)
    halves(2)
    forward(1, 3)
    w_core_arrived(2)
    give_back(0, 2)
    loads[5].wait()
    project(pair, 0, 0)
    halves(3)
    rows_arrived(1, 0)
    w_core_arrived(3)
    give_back(0, 3)
    passed(1)
    for i in (1, 2, 3):
        give_back(1, i)
    project(pair, 0, 1)
    keep = pltpu.make_async_copy(out_ref.at[0], out_hbm.at[tile_rows(pair), :], load_sem.at[0])
    keep.start()

    for i in (1, 2, 3):
        w_z(i).wait_send()
        for o in (0, 1, 2, 3):
            w_core(i, o).wait_send()
        for o in (1, 2, 3):
            w_first(i, o).wait_send()
        for d, o in ((0, 1), (1, 3)):
            w_second(i, o).wait_send()
            w_relay(i, d).wait_send()
    for t in (0, 1):
        for k in (1, 2, 3):
            pass_on(t, k).wait_send()
        for k in (0, 1, 2, 3):
            to_pair(t, k).wait_send()
    to_others(lambda i: send_part(i).wait_send(), 0, 8)
    to_others(lambda i: send_sum(i).wait_send(), 0, 8)
    keep.wait()
    for t in (0, 1):
        for i in (1, 2, 3):
            back(t, i).wait_send()
            back_arrived(t, i)


def local(query_rows, key_rows, value_rows, frequencies, norm_gain, out_weight):
    anywhere = pl.BlockSpec(memory_space=pl.ANY)
    operands = [
        pltpu.with_memory_space_constraint(operand, pltpu.HBM)
        for operand in (query_rows, key_rows, value_rows, frequencies, norm_gain, out_weight)
    ]
    return pl.pallas_call(
        kernel,
        out_shape=jax.ShapeDtypeStruct((ROWS, 512), BF16),
        in_specs=[anywhere] * 6,
        out_specs=anywhere,
        scratch_shapes=[
            pltpu.VMEM((ROWS, 512), BF16),
            pltpu.VMEM((ROWS, 512), BF16),
            pltpu.VMEM((ROWS, 512), BF16),
            pltpu.VMEM((HEADS, HDIM, HDIM), BF16),
            pltpu.VMEM((512,), BF16),
            pltpu.VMEM((4, 4096, 512), BF16),
            pltpu.VMEM((HEADS, ROWS, FEATS), BF16),
            pltpu.VMEM((HEADS, ROWS, FEATS), BF16),
            pltpu.VMEM((2, 512, FEATS), F32),
            pltpu.VMEM((ROWS, 512), F32),
            pltpu.VMEM((ROWS, 512), BF16),
            pltpu.VMEM((RING, TILE, 512), BF16),
            pltpu.VMEM((HALF, 512), F32),
            pltpu.VMEM((4, TILE, 512), BF16),
            pltpu.VMEM((512, FEATS), BF16),
            pltpu.VMEM((SEATS, PART, FEATS), BF16),
            pltpu.VMEM((PART, FEATS), BF16),
            pltpu.VMEM((3, PART, FEATS), BF16),
            pltpu.VMEM((SEATS, PART, FEATS), BF16),
            pltpu.VMEM((2, 512, FEATS), BF16),
            pltpu.SemaphoreType.DMA((6,)),
            pltpu.SemaphoreType.DMA((2, SEATS)),
            pltpu.SemaphoreType.DMA((2, 3)),
            pltpu.SemaphoreType.DMA((2, SEATS)),
            pltpu.SemaphoreType.DMA((2, 3)),
            pltpu.SemaphoreType.DMA((3, 2, 3)),
            pltpu.SemaphoreType.DMA((3, 2, 3)),
            pltpu.SemaphoreType.DMA((3, 2, 2)),
            pltpu.SemaphoreType.DMA((3, 2, 4)),
            pltpu.SemaphoreType.DMA((2, 2, 4)),
            pltpu.SemaphoreType.DMA((2, 2, 3)),
            pltpu.SemaphoreType.DMA((2, 2, 3)),
        ],
        compiler_params=pltpu.CompilerParams(
            collective_id=0, has_side_effects=True, vmem_limit_bytes=50 * 2**20
        ),
        cost_estimate=pl.CostEstimate(
            flops=7 * 10**9, bytes_accessed=9 * 2**20, transcendentals=0
        ),
    )(*operands)


def solution(mesh):
    return jax.shard_map(
        local,
        mesh=mesh,
        in_specs=(
            P("ctx", "head"),
            P("ctx", "head"),
            P("ctx", "head"),
            P("head", None, None),
            P("head"),
            P(None, "head"),
        ),
        out_specs=P("ctx", "head"),
        check_vma=False,
    )
```
